256 devices in a mesh: chol: 16 (over x, y), walker: 8 (over z), orb: 2 (over core).
Axes of the slice: x: 4, y: 4, z: 8, core: 2. Of those that a mesh axis runs over, the one named last changes fastest.
Arguments:
- chol_vals: bfloat16 [4096, 4, 64, 128], P('chol', 'orb'), may hold values from -0.05 to 0.05, as said below
- chol_cols: int32 [4096, 4, 2], P('chol', 'orb'), may hold values from 0 to 4, as said below
- greens: bfloat16 [256, 256, 256], P('walker', 'orb'), may hold values from -0.75 to 0.75
- walkers: bfloat16 [256, 256, 128], P('walker', 'orb'), may hold values from -6 to 6
- fields: float32 [4096, 256], P('chol', 'walker'), may hold values from -6 to 6
Outputs:
- new_walkers: bfloat16 [256, 256, 128], P('walker', 'orb')
- energy: float32 [256], P('walker')
The draws below stay inside these ranges and needn't reach their ends.
Inputs may be any that keep to these rules, and one draw needn't show every extreme that they name: `chol_cols`: for every vector g and block row r, slot 0 holds r; the other slots hold distinct block columns different from r, or 4 for an empty slot. `chol_vals`: values of the stored blocks; entries in empty slots are not used.
All inputs are finite; a program needn't handle non-finite values.
Results may differ from the reference program's by a relative error of at most 0.0055.
Values may be sent and summed in bfloat16 or wider, within the bound.
A program may use at most 128 MiB of HBM per device.

```python
import jax
import jax.numpy as jnp
from jax import lax

NORB = 256
NOCC = 128
BLOCK = 64
SLOTS = 2
TAYLOR = 4
VEC_DEV = 256
ROWBLK = 4
NVEC = 4096
WALKERS = 256


def draw_chol_vals(key, part):
    array_shape = (NVEC, ROWBLK, BLOCK, SLOTS * BLOCK)
    vector_index = jnp.arange(NVEC, dtype=jnp.float32)
    decay_scale = 0.0075 * jnp.exp(-1.4 * vector_index / NVEC)
    base_draw = jnp.clip(jax.random.normal(key, array_shape, jnp.float32), -6.0, 6.0)
    return (base_draw * decay_scale[:, None, None, None]).astype(jnp.bfloat16)


def draw_chol_cols(key, part):
    first_key = jax.random.fold_in(key, 11)
    second_key = jax.random.fold_in(key, 23)
    scores = jax.random.randint(first_key, (NVEC, ROWBLK, ROWBLK), 0, 1 << 20) * ROWBLK
    scores = scores + jnp.arange(ROWBLK, dtype=jnp.int32)
    diagonal_mask = jnp.arange(ROWBLK)[:, None] == jnp.arange(ROWBLK)[None, :]
    scores = jnp.where(diagonal_mask[None], -1, scores)
    ranked = jnp.argsort(scores, axis=-1)[..., :SLOTS].astype(jnp.int32)
    empty_slot = jax.random.randint(second_key, (NVEC, ROWBLK, SLOTS), 0, 3) == 0
    slot_zero = jnp.arange(SLOTS)[None, None, :] == 0
    return jnp.where(empty_slot & jnp.logical_not(slot_zero), ROWBLK, ranked).astype(jnp.int32)


def block_scale(key, dims, cuts, smallest, top_value):
    factor_of, own = 1.0, jax.random.fold_in(key, 6)
    for axis_at, parts in cuts:
        draws = jnp.exp(jax.random.uniform(jax.random.fold_in(own, axis_at), (parts,), jnp.float32, smallest / len(cuts), top_value / len(cuts)))
        factor_of = factor_of * jnp.repeat(draws, dims[axis_at] // parts).reshape([-1 if axis == axis_at else 1 for axis in range(len(dims))])
    return factor_of


def noise(rng, dims, deviation, limit, split=(), kind=jnp.bfloat16):
    array = deviation * jax.random.normal(rng, dims, jnp.float32)
    if split:
        array = array * block_scale(rng, dims, split, -0.22, 0.18)
    return jnp.clip(array, -limit, limit).astype(kind)


def setup_inputs(seed: int = 0) -> dict:
    streams_of = jax.random.split(jax.random.key(seed), 6)
    chol_vals = draw_chol_vals(jax.random.fold_in(streams_of[5], 71), 0)
    chol_cols = draw_chol_cols(jax.random.fold_in(streams_of[5], 71), 0)
    greens = noise(streams_of[2], (WALKERS, NORB, NORB), 0.125, 0.75, ((0, 8), (1, 2)))
    walkers = noise(streams_of[3], (WALKERS, NORB, NOCC), 1.0, 6.0, ((0, 8), (1, 2)))
    fields = noise(streams_of[4], (NVEC, WALKERS), 1.0, 6.0, ((0, 16), (1, 8)), jnp.float32)
    return dict(chol_vals=chol_vals, chol_cols=chol_cols, greens=greens, walkers=walkers, fields=fields)


def dense_rows(values, columns):
    vectors = values.shape[0]
    pieces = values.astype(jnp.float32).reshape(vectors, ROWBLK, BLOCK, SLOTS, BLOCK)
    onehot = (columns[..., None] == jnp.arange(ROWBLK, dtype=jnp.int32)).astype(jnp.float32)
    placed = jnp.einsum('grsc,grisj->gricj', onehot, pieces, precision=lax.Precision.HIGHEST)
    return placed.reshape(vectors, NORB * NORB)


def reference(chol_vals, chol_cols, greens, walkers, fields):
    groups = NVEC // VEC_DEV
    value_groups = chol_vals.reshape(groups, VEC_DEV, ROWBLK, BLOCK, SLOTS * BLOCK)
    column_groups = chol_cols.reshape(groups, VEC_DEV, ROWBLK, SLOTS)
    green_flat = greens.astype(jnp.float32).reshape(WALKERS, NORB * NORB)

    def bias_group(pair):
        matrix = dense_rows(pair[0], pair[1])
        return jnp.dot(matrix, green_flat.T, precision=lax.Precision.HIGHEST)

    force_bias = lax.map(bias_group, (value_groups, column_groups)).reshape(NVEC, WALKERS)
    energy = 0.5 * jnp.sum(force_bias * force_bias, axis=0)
    shifted = lax.optimization_barrier((fields - force_bias).astype(jnp.bfloat16))
    shift_groups = shifted.astype(jnp.float32).reshape(groups, VEC_DEV, WALKERS)

    def add_group(total, triple):
        matrix = dense_rows(triple[0], triple[1])
        return total + jnp.dot(triple[2].T, matrix, precision=lax.Precision.HIGHEST), None

    total, unused = lax.scan(add_group, jnp.zeros((WALKERS, NORB * NORB), jnp.float32),
                             (value_groups, column_groups, shift_groups))
    step_factor = 72.0 / float(NVEC * BLOCK) ** 0.5
    potential = lax.optimization_barrier((step_factor * total).reshape(WALKERS, NORB, NORB).astype(jnp.bfloat16))
    potential = potential.astype(jnp.float32)
    series_term = walkers
    series_sum = jnp.zeros((WALKERS, NORB, NOCC), jnp.float32)
    for degree in range(1, TAYLOR + 1):
        product = jnp.einsum('wij,wja->wia', potential, series_term.astype(jnp.float32),
                             precision=lax.Precision.HIGHEST)
        series_term = lax.optimization_barrier((product / degree).astype(jnp.bfloat16))
        series_sum = series_sum + series_term.astype(jnp.float32)
    new_walkers = (walkers.astype(jnp.float32) + series_sum).astype(jnp.bfloat16)
    return new_walkers, energy
```

```python
import functools

import jax
import jax.numpy as jnp
from jax import lax
from jax.experimental import pallas as pl
from jax.experimental.pallas import tpu as pltpu
from jax.sharding import PartitionSpec as P

NORB = 256
NOCC = 128
BLOCK = 64
TAYLOR = 4
SIDE = 4
F32 = jnp.float32
BF16 = jnp.bfloat16
MESH = pl.DeviceIdType.MESH
HALF = 64


def swap_halves(x):
    return jnp.concatenate([x[:, BLOCK:], x[:, :BLOCK]], axis=1)


def kernel(
    step_factor, v_hbm, cols_hbm, g_hbm, w_hbm, f_hbm, out_hbm, e_ref,
    vbuf, vt, gbuf, gp, cbuf, fbuf, wbuf, tbuf, fx, fxr,
    pp, opp1, fin1, s1, opp2, fin2, own2, pot, nw, gathered, esend, ebuf,
    lsem, ssem, rsem, osem,
):
    chip = lax.axis_index("chol")
    core = lax.axis_index("orb")
    other = 1 - core
    px, py = chip // SIDE, chip % SIDE

    def chip_at(dx, dy):
        return ((px + dx) % SIDE) * SIDE + (py + dy) % SIDE

    def chip_of(h, da, db):
        return chip_at(da, db) if h == 0 else chip_at(db, da)

    def walker(h, da, db):
        return 2 * chip_of(h, da, db) + h

    def dev(c, k):
        return {"chol": c, "orb": k}

    sends = []
    count = [0]

    def slots(n=1):
        count[0] += n
        return count[0] - n

    def remote(src, dst, to, sidx, ridx):
        return pltpu.make_async_remote_copy(
            src_ref=src, dst_ref=dst, send_sem=ssem.at[sidx], recv_sem=rsem.at[ridx],
            device_id=to, device_id_type=MESH,
        )

    def send(src, dst, to, ridx=None):
        sidx = slots()
        ridx = sidx if ridx is None else ridx
        c = remote(src, dst, to, sidx, ridx)
        c.start()
        sends.append(c)
        return ridx

    def arrive(dst, ridx):
        remote(dst, dst, dev(chip, other), ridx, ridx).wait_recv()

    barrier = pltpu.get_barrier_semaphore()
    partners = [dev(chip, other)]
    for dx, dy in ((1, 0), (3, 0), (0, 1), (0, 3)):
        partners += [dev(chip_at(dx, dy), core), dev(chip_at(dx, dy), other)]
    for dx, dy in ((2, 0), (0, 2)):
        partners.append(dev(chip_at(dx, dy), core))
    for to in partners:
        pl.semaphore_signal(barrier, inc=1, device_id=to, device_id_type=MESH)

    gcopy = pltpu.make_async_copy(g_hbm, gbuf, lsem.at[8])
    gcopy.start()
    vcopies = []
    for n in range(8):
        r, ii = divmod(n, 4)
        c = pltpu.make_async_copy(v_hbm.at[:, r, pl.ds(ii * 16, 16), :], vbuf.at[n], lsem.at[n])
        c.start()
        vcopies.append(c)
    fcopy = pltpu.make_async_copy(f_hbm, fbuf, lsem.at[9])
    fcopy.start()
    ccopy = pltpu.make_async_copy(cols_hbm, cbuf, lsem.at[10])
    ccopy.start()
    wcopy = pltpu.make_async_copy(w_hbm.at[pl.ds(2 * chip, 2)], wbuf, lsem.at[11])
    wcopy.start()

    gcopy.wait()
    low = lax.broadcasted_iota(jnp.int32, (16, 128), 1) < BLOCK
    own_at = pl.multiple_of(core * 128, 128)
    far_at = pl.multiple_of(other * 128, 128)
    for r in range(2):

        @pl.loop(0, 8)
        def _(n):
            w0 = pl.multiple_of((n % 2) * 16, 16)
            i0 = pl.multiple_of((n // 2) * 16, 16)
            rows = pl.ds(r * 64 + i0, 16)
            near = jnp.swapaxes(gbuf[pl.ds(w0, 16), rows, pl.ds(own_at, 128)], 0, 1)
            far = jnp.swapaxes(gbuf[pl.ds(w0, 16), rows, pl.ds(far_at, 128)], 0, 1)
            for i in range(16):
                a, b = near[i], far[i]
                if r == 1:
                    a = swap_halves(a)
                z = jnp.zeros_like(a)
                choices = (jnp.where(low, a, z), a, jnp.where(low, a, swap_halves(b)), jnp.where(low, a, b))
                for c, val in enumerate(choices):
                    gp[r, pl.ds(c * 32 + w0, 16), pl.ds(pl.multiple_of(i0 * 128, 128) + i * 128, 128)] = val

    acc = [None, None]
    for n in range(8):
        r, ii = divmod(n, 4)
        vcopies[n].wait()

        @pl.loop(0, 16)
        def _(gg):
            g0 = pl.multiple_of(gg * 16, 16)
            y = jnp.swapaxes(vbuf[n, pl.ds(g0, 16), :, :], 0, 1)
            for i in range(16):
                vt[r, pl.ds(g0, 16), (ii * 16 + i) * 128:(ii * 16 + i + 1) * 128] = y[i]

        ks = slice(ii * 2048, (ii + 1) * 2048)
        d = lax.dot_general(gp[r, :, ks], vt[r, :, ks], (((1,), (1,)), ((), ())), preferred_element_type=F32)
        acc[r] = d if acc[r] is None else acc[r] + d
    fcopy.wait()
    ccopy.wait()
    wcopy.wait()
    masks = []
    partial = jnp.zeros((32, 256), F32)
    for r in range(2):
        code = cbuf[r, 1:2, :]
        wanted = (4, 2 * core + (1 - r), 2 * other, 2 * other + 1)
        ms = [code == k for k in wanted]
        masks.append(ms)
        for c in range(4):
            partial = partial + jnp.where(ms[c], acc[r][c * 32:(c + 1) * 32], 0.0)
    fx[...] = partial
    tbuf[core] = wbuf[core]
    pl.semaphore_wait(barrier, len(partners))
    fi = send(fx, fxr, dev(chip, other))
    wi = send(wbuf.at[other], tbuf.at[core], dev(chip, other))
    arrive(fxr, fi)
    bias = partial + fxr[...]
    shifted = fbuf[...] - bias

    local = 0.5 * jnp.sum(bias * bias, axis=1, keepdims=True)
    diag = lax.broadcasted_iota(jnp.int32, (32, 128), 0) == lax.broadcasted_iota(jnp.int32, (32, 128), 1)
    row = jnp.sum(jnp.where(diag, local, 0.0), axis=0, keepdims=True)
    esend[0] = jnp.broadcast_to(row, (8, 128))
    ebuf[0, px] = jnp.broadcast_to(row, (8, 128))
    ex = slots(SIDE)
    for d in (1, 2, 3):
        send(esend.at[0], ebuf.at[0, px], dev(chip_at(d, 0), core), ex + px)

    lo32 = lax.broadcasted_iota(jnp.int32, (32, 128), 1) < BLOCK
    order = (2, 1, 3, 0)
    o1 = {}
    f1 = {}
    for r in range(2):
        parts = [shifted] + [jnp.where(masks[r][c], shifted, 0.0) for c in (1, 2, 3)]
        lhs = jnp.concatenate(parts, axis=0).astype(BF16)

        @pl.loop(0, 4)
        def _(ii):
            k0 = pl.multiple_of(ii * 2048, 2048)
            o = jnp.dot(lhs, vt[r, :, pl.ds(k0, 2048)], preferred_element_type=F32)
            x0, x1 = [], []
            for i in range(16):
                t = o[:, i * 128:(i + 1) * 128]
                x0.append(jnp.where(lo32, t[0:32], t[32:64]).astype(BF16))
                x1.append(jnp.where(lo32, pltpu.roll(t[64:96], 64, 1), t[96:128]).astype(BF16))
            i0 = pl.multiple_of(r * 64 + ii * 16, 16)
            for wh in range(2):
                for side, x in ((0, x0), (1, x1)):
                    s = jnp.stack([q[wh * 16:(wh + 1) * 16] for q in x], axis=0)
                    pp[wh * 16:(wh + 1) * 16, pl.ds(i0, 16), side * 128:(side + 1) * 128] = jnp.swapaxes(s, 0, 1)

        rows = pl.ds(r * HALF, HALF)
        step = 1 if r == 0 else 3
        for d in order:
            for h in range(2):
                o1[h, d, r] = send(pp.at[walker(h, 2, d), rows], opp1.at[h, d, r], dev(chip_of(h, step, 0), core))
        for d in order:
            for h in range(2):
                f1[h, d, 1 - r, r] = send(
                    pp.at[walker(h, 4 - step, d), rows], fin1.at[h, d, 1 - r, rows], dev(chip_of(h, 4 - step, 0), core)
                )

    for d in (1, 2, 3):
        qx = (px + d) % SIDE
        arrive(ebuf.at[0, qx], ex + qx)
    row = (ebuf[0, 0] + ebuf[0, 1]) + (ebuf[0, 2] + ebuf[0, 3])
    esend[1] = row
    ebuf[1, py] = row
    ey = slots(SIDE)
    for d in (1, 2, 3):
        send(esend.at[1], ebuf.at[1, py], dev(chip_at(0, d), core), ey + py)

    def forward1(d):
        for h in range(2):
            for r in range(2):
                rows = pl.ds(r * HALF, HALF)
                step = 1 if r == 0 else 3
                arrive(opp1.at[h, d, r], o1[h, d, r])
                w = walker(h, step, d)
                pp[w, rows] = (pp[w, rows].astype(F32) + opp1[h, d, r].astype(F32)).astype(BF16)
                f1[h, d, r, r] = send(pp.at[w, rows], fin1.at[h, d, r, rows], dev(chip_of(h, step, 0), core))

    def finish1(d):
        for h in range(2):
            for s in range(2):
                for r in range(2):
                    arrive(fin1.at[h, d, s, pl.ds(r * HALF, HALF)], f1[h, d, s, r])
            s1[h, d] = (
                pp[walker(h, 0, d)].astype(F32) + fin1[h, d, 0].astype(F32) + fin1[h, d, 1].astype(F32)
            ).astype(BF16)

    forward1(2)
    forward1(1)
    finish1(2)
    o2 = {}
    for h in range(2):
        for r in range(2):
            step = 1 if r == 0 else 3
            o2[h, r] = send(s1.at[h, 2, pl.ds(r * HALF, HALF)], opp2.at[h, r], dev(chip_of(h, 0, step), core))
    forward1(3)
    forward1(0)
    f2 = slots(8)
    for d, s in ((1, 0), (3, 1)):
        finish1(d)
        rows = pl.ds((1 - s) * HALF, HALF)
        for h in range(2):
            send(s1.at[h, d, rows], fin2.at[core, s, rows], dev(chip_of(h, 0, d), h), f2 + core * 4 + s * 2 + (1 - s))
    for d, s in ((1, 0), (3, 1)):
        rows = pl.ds(s * HALF, HALF)
        for h in range(2):
            arrive(opp2.at[h, s], o2[h, s])
            s1[h, d, rows] = (s1[h, d, rows].astype(F32) + opp2[h, s].astype(F32)).astype(BF16)
            send(s1.at[h, d, rows], fin2.at[core, s, rows], dev(chip_of(h, 0, d), h), f2 + core * 4 + s * 2 + s)
    finish1(0)
    own2[core] = s1[core, 0]
    oi = send(s1.at[other, 0], own2.at[core], dev(chip, other))

    for d in (1, 2, 3):
        qy = (py + d) % SIDE
        arrive(ebuf.at[1, qy], ey + qy)
    row = (ebuf[1, 0] + ebuf[1, 1]) + (ebuf[1, 2] + ebuf[1, 3])
    e_ref[...] = row[0:1, 0:32]

    arrive(own2.at[other], oi)
    for o in range(2):
        for s in range(2):
            for r in range(2):
                arrive(fin2.at[o, s, pl.ds(r * HALF, HALF)], f2 + o * 4 + s * 2 + r)
    for o in range(2):
        full = step_factor * (own2[o].astype(F32) + fin2[o, 0].astype(F32) + fin2[o, 1].astype(F32))
        near, far = full[:, :128], full[:, 128:]
        near = jnp.concatenate([near[:BLOCK], pltpu.roll(near[BLOCK:], BLOCK, 1)], axis=0)
        pair = [near, far] if o == 0 else [far, near]
        pot[o * 128:(o + 1) * 128, :] = jnp.concatenate(pair, axis=1).astype(BF16)
    arrive(tbuf.at[other], wi)
    start = tbuf[...].reshape(NORB, NOCC)
    term = start
    total = jnp.zeros((NORB, NOCC), F32)
    for degree in range(1, TAYLOR + 1):
        product = jnp.dot(pot[...], term, preferred_element_type=F32)
        term = (product / degree).astype(BF16)
        total = total + term.astype(F32)
    nw[...] = (start.astype(F32) + total).astype(BF16).reshape(2, 128, NOCC)

    mine = 2 * chip + core
    g1 = slots(4)
    for n, s in enumerate((1, 3)):
        for o in range(2):
            send(nw.at[o], gathered.at[mine], dev(chip_at(core * s, other * s), o), g1 + core * 2 + n)
    gi = send(nw.at[other], gathered.at[mine], dev(chip, other))
    gathered[mine] = nw[core]
    first, second = pl.ds(0, HALF), pl.ds(HALF, HALF)
    g2 = {}
    g3 = {}
    g4 = {}

    def done(w):
        pltpu.make_async_copy(gathered.at[w], out_hbm.at[w], osem).start()

    def spread(h, db):
        w = walker(h, 0, db)
        for n, step in enumerate((1, 3)):
            g3[h, db, n] = send(gathered.at[w], gathered.at[w], dev(chip_of(h, step, 0), core))
        done(w)

    arrive(gathered.at[2 * chip + other], gi)
    for h in range(2):
        spread(h, 0)
    for h in range(2):
        for n, (db, step, rows) in enumerate(((3, 1, first), (1, 3, second))):
            w = walker(h, 0, db)
            arrive(gathered.at[w], g1 + h * 2 + n)
            g2[h, n] = send(gathered.at[w, rows], gathered.at[w, rows], dev(chip_of(h, 0, step), core))
            spread(h, db)

    def pass_on(h, db):
        for n, (da, step, rows) in enumerate(((3, 1, first), (1, 3, second))):
            w = walker(h, da, db)
            arrive(gathered.at[w], g3[h, db, n])
            g4[h, db, n] = send(gathered.at[w, rows], gathered.at[w, rows], dev(chip_of(h, step, 0), core))
            done(w)

    for h in range(2):
        pass_on(h, 0)
    for h in range(2):
        for n, rows in enumerate((first, second)):
            arrive(gathered.at[walker(h, 0, 2), rows], g2[h, n])
        spread(h, 2)
    for db in (3, 1, 2):
        for h in range(2):
            pass_on(h, db)
    for db in (0, 3, 1, 2):
        for h in range(2):
            w = walker(h, 2, db)
            for n, rows in enumerate((first, second)):
                arrive(gathered.at[w, rows], g4[h, db, n])
            done(w)
    for c in sends:
        c.wait_send()
    pltpu.make_async_copy(gathered, out_hbm, osem).wait()
    assert count[0] <= SEMS, count[0]


SEMS = 160


def per_device(chol_vals, chol_cols, greens, walkers, fields):
    vectors = chol_vals.shape[0]
    step_factor = 72.0 / float(vectors * lax.axis_size("chol") * BLOCK) ** 0.5
    vmem = pltpu.VMEM
    any_space = pl.BlockSpec(memory_space=pl.ANY)
    new_walkers, energy = pl.pallas_call(
        functools.partial(kernel, step_factor),
        out_shape=(
            jax.ShapeDtypeStruct((32, 128, NOCC), BF16),
            jax.ShapeDtypeStruct((1, 32), F32),
        ),
        in_specs=[any_space] * 5,
        out_specs=(any_space, pl.BlockSpec(memory_space=vmem)),
        scratch_shapes=[
            vmem((8, 256, 16, 128), BF16),
            vmem((2, 256, 64 * 128), BF16),
            vmem((32, 128, 256), BF16),
            vmem((2, 128, 64 * 128), BF16),
            vmem((2, 2, 256), jnp.int32),
            vmem((32, 256), F32),
            vmem((2, 128, NOCC), BF16),
            vmem((2, 128, NOCC), BF16),
            vmem((32, 256), F32),
            vmem((32, 256), F32),
            vmem((32, 128, 256), BF16),
            vmem((2, 4, 2, HALF, 256), BF16),
            vmem((2, 4, 2, 128, 256), BF16),
            vmem((2, 4, 128, 256), BF16),
            vmem((2, 2, HALF, 256), BF16),
            vmem((2, 2, 128, 256), BF16),
            vmem((2, 128, 256), BF16),
            vmem((NORB, NORB), BF16),
            vmem((2, 128, NOCC), BF16),
            vmem((32, 128, NOCC), BF16),
            vmem((2, 8, 128), F32),
            vmem((2, SIDE, 8, 128), F32),
            pltpu.SemaphoreType.DMA((12,)),
            pltpu.SemaphoreType.DMA((SEMS,)),
            pltpu.SemaphoreType.DMA((SEMS,)),
            pltpu.SemaphoreType.DMA,
        ],
        compiler_params=pltpu.CompilerParams(
            collective_id=0, has_side_effects=True, vmem_limit_bytes=56 << 20
        ),
    )(chol_vals, chol_cols.transpose(1, 2, 0), greens, walkers, fields.T)
    return new_walkers, energy.reshape(32)


def solution(mesh):
    in_specs = (
        P("chol", "orb", None, None),
        P("chol", "orb", None),
        P("walker", "orb", None),
        P("walker", "orb", None),
        P("chol", "walker"),
    )
    out_specs = (P("walker", "orb", None), P("walker"))
    return jax.shard_map(
        per_device, mesh=mesh, in_specs=in_specs, out_specs=out_specs, check_vma=False
    )
```

```python
import functools

import jax
import jax.numpy as jnp
from jax import lax
from jax.experimental import pallas as pl
from jax.experimental.pallas import tpu as pltpu
from jax.sharding import PartitionSpec as P

NORB = 256
NOCC = 128
BLOCK = 64
TAYLOR = 4
SIDE = 4
F32 = jnp.float32
BF16 = jnp.bfloat16
MESH = pl.DeviceIdType.MESH
HALF = 64


def swap_halves(x):
    return jnp.concatenate([x[:, BLOCK:], x[:, :BLOCK]], axis=1)


def kernel(
    step_factor, v_hbm, cols_hbm, g_hbm, w_hbm, f_hbm, out, e_ref,
    vbuf, vt, gbuf, gp, cbuf, fbuf, wbuf, tbuf, fx, fxr,
    pp, opp1, fin1, s1, last, pot, nw, esend, ebuf,
    lsem, ssem, rsem,
):
    chip = lax.axis_index("chol")
    core = lax.axis_index("orb")
    other = 1 - core
    px, py = chip // SIDE, chip % SIDE

    def chip_at(dx, dy):
        return ((px + dx) % SIDE) * SIDE + (py + dy) % SIDE

    def chip_of(h, da, db):
        return chip_at(da, db) if h == 0 else chip_at(db, da)

    def walker(h, da, db):
        return 2 * chip_of(h, da, db) + h

    def dev(c, k):
        return {"chol": c, "orb": k}

    used = [0]

    def slots(n=1):
        used[0] += n
        return used[0] - n

    def remote(src, dst, to, ridx, small=0):
        return pltpu.make_async_remote_copy(
            src_ref=src, dst_ref=dst, send_sem=ssem.at[small], recv_sem=rsem.at[ridx],
            device_id=to, device_id_type=MESH,
        )

    def send(src, dst, to, ridx, small=0):
        remote(src, dst, to, ridx, small).start()

    def arrive(dst, ridx):
        remote(dst, dst, dev(chip, other), ridx).wait_recv()

    barrier = pltpu.get_barrier_semaphore()
    partners = [dev(chip, other)]
    for dx, dy in ((1, 0), (3, 0), (2, 0), (0, 1), (0, 3), (0, 2)):
        partners += [dev(chip_at(dx, dy), core), dev(chip_at(dx, dy), other)]
    for to in partners:
        pl.semaphore_signal(barrier, inc=1, device_id=to, device_id_type=MESH)

    def load_g(n):
        rows = pl.ds(n * 16, 16)
        return pltpu.make_async_copy(g_hbm.at[:, rows, :], gbuf.at[:, rows, :], lsem.at[8 + n])

    def load_v(r, ii):
        n = r * 4 + ii
        return pltpu.make_async_copy(v_hbm.at[:, r, pl.ds(ii * 16, 16), :], vbuf.at[n], lsem.at[n])

    for r in range(2):
        for ii in range(4):
            load_g(r * 4 + ii).start()
            load_v(r, ii).start()
    fcopy = pltpu.make_async_copy(f_hbm, fbuf, lsem.at[16])
    fcopy.start()
    ccopy = pltpu.make_async_copy(cols_hbm, cbuf, lsem.at[17])
    ccopy.start()
    wcopy = pltpu.make_async_copy(w_hbm.at[pl.ds(2 * chip, 2)], wbuf, lsem.at[18])
    wcopy.start()

    low = lax.broadcasted_iota(jnp.int32, (16, 128), 1) < BLOCK
    own_at = pl.multiple_of(core * 128, 128)
    far_at = pl.multiple_of(other * 128, 128)
    for r in range(2):

        @pl.loop(0, 4)
        def _(ii):
            load_g(r * 4 + ii).wait()
            load_v(r, ii).wait()
            rows = pl.ds(pl.multiple_of(r * 64 + ii * 16, 16), 16)
            k0 = pl.multiple_of(ii * 2048, 2048)
            for w0 in (0, 16):
                near = jnp.swapaxes(gbuf[w0:w0 + 16, rows, pl.ds(own_at, 128)], 0, 1)
                far = jnp.swapaxes(gbuf[w0:w0 + 16, rows, pl.ds(far_at, 128)], 0, 1)
                for i in range(16):
                    a, b = near[i], far[i]
                    if r == 1:
                        a = swap_halves(a)
                    z = jnp.zeros_like(a)
                    choices = (jnp.where(low, a, z), a, jnp.where(low, a, swap_halves(b)), jnp.where(low, a, b))
                    for c, val in enumerate(choices):
                        gp[r, c * 32 + w0:c * 32 + w0 + 16, pl.ds(k0 + i * 128, 128)] = val
            for g0 in range(0, 256, 16):
                y = jnp.swapaxes(vbuf[r * 4 + ii, g0:g0 + 16, :, :], 0, 1)
                for i in range(16):
                    vt[r, g0:g0 + 16, pl.ds(k0 + i * 128, 128)] = y[i]

    fcopy.wait()
    ccopy.wait()
    wcopy.wait()
    masks = []
    partial = jnp.zeros((32, 256), F32)
    for r in range(2):
        acc = lax.dot_general(vt[r], gp[r], (((1,), (1,)), ((), ())), preferred_element_type=F32).T
        code = cbuf[r, 1:2, :]
        wanted = (4, 2 * core + (1 - r), 2 * other, 2 * other + 1)
        ms = [code == k for k in wanted]
        masks.append(ms)
        for c in range(4):
            partial = partial + jnp.where(ms[c], acc[c * 32:(c + 1) * 32], 0.0)
    fx[...] = partial
    tbuf[core] = wbuf[core]
    fi, wi = slots(), slots()
    pl.semaphore_wait(barrier, len(partners))
    send(fx, fxr, dev(chip, other), fi)
    send(wbuf.at[other], tbuf.at[core], dev(chip, other), wi)
    arrive(fxr, fi)
    bias = partial + fxr[...]
    shifted = fbuf[...] - bias

    local = 0.5 * jnp.sum(bias * bias, axis=1, keepdims=True)
    diag = lax.broadcasted_iota(jnp.int32, (32, 128), 0) == lax.broadcasted_iota(jnp.int32, (32, 128), 1)
    row = jnp.sum(jnp.where(diag, local, 0.0), axis=0, keepdims=True)
    esend[0] = jnp.broadcast_to(row, (8, 128))
    ex, ey = slots(), slots()
    for d in (1, 2, 3):
        send(esend.at[0], ebuf.at[0, d], dev(chip_at(d, 0), core), ex, 1)

    lo32 = lax.broadcasted_iota(jnp.int32, (32, 128), 1) < BLOCK
    order = (2, 1, 3, 0)
    o1 = {(h, d, r): slots() for h in range(2) for d in range(4) for r in range(2)}
    f1 = {(h, d): slots() for h in range(2) for d in (1, 2, 3)}
    fl = slots()

    def rows_of(r):
        return pl.ds(r * HALF, HALF)

    def way(r):
        return 1 if r == 0 else 3

    def send_opp(d, r):
        for h in range(2):
            send(pp.at[walker(h, 2, d), rows_of(r)], opp1.at[h, d, r], dev(chip_of(h, way(r), 0), core), o1[h, d, r])

    def send_target(d, r, step):
        s = 0 if step == 1 else 1
        for h in range(2):
            src = pp.at[walker(h, step, d), rows_of(r)]
            if d == 0:
                send(src, last.at[core * 5 + s, rows_of(r)], dev(chip_of(h, step, 0), h), fl)
            else:
                send(src, fin1.at[h, d, s, rows_of(r)], dev(chip_of(h, step, 0), core), f1[h, d])

    def add_opp(d, r):
        for h in range(2):
            arrive(opp1.at[h, d, r], o1[h, d, r])
            w = walker(h, way(r), d)
            pp[w, rows_of(r)] = (pp[w, rows_of(r)].astype(F32) + opp1[h, d, r].astype(F32)).astype(BF16)

    for r in range(2):
        parts = [shifted] + [jnp.where(masks[r][c], shifted, 0.0) for c in (1, 2, 3)]
        lhs = jnp.concatenate(parts, axis=0).astype(BF16)

        @pl.loop(0, 4)
        def _(ii):
            k0 = pl.multiple_of(ii * 2048, 2048)
            o = jnp.dot(lhs, vt[r, :, pl.ds(k0, 2048)], preferred_element_type=F32)
            x0, x1 = [], []
            for i in range(16):
                t = o[:, i * 128:(i + 1) * 128]
                x0.append(jnp.where(lo32, t[0:32], t[32:64]).astype(BF16))
                x1.append(jnp.where(lo32, pltpu.roll(t[64:96], 64, 1), t[96:128]).astype(BF16))
            i0 = pl.multiple_of(r * 64 + ii * 16, 16)
            for wh in range(2):
                for side, x in ((0, x0), (1, x1)):
                    s = jnp.stack([q[wh * 16:(wh + 1) * 16] for q in x], axis=0)
                    pp[wh * 16:(wh + 1) * 16, pl.ds(i0, 16), side * 128:(side + 1) * 128] = jnp.swapaxes(s, 0, 1)

        for d in order:
            send_opp(d, r)
        if r == 0:
            send_target(2, 0, 3)
            send_target(1, 0, 3)
    send_target(2, 1, 1)
    send_target(1, 1, 1)
    send(pp.at[2 * chip + other], last.at[10], dev(chip, other), fl)

    arrive(ebuf.at[0, pl.ds(1, 3)], ex)
    ebuf[0, 0] = esend[0]
    row = ordered_sum(ebuf, 0, px)
    esend[1] = row
    for d in (1, 2, 3):
        send(esend.at[1], ebuf.at[1, d], dev(chip_at(0, d), core), ey, 1)

    for n, d in enumerate(order):
        for r in range(2):
            add_opp(d, r)
            send_target(d, r, way(r))
        if n + 2 < 4:
            send_target(order[n + 2], 1, 1)
            send_target(order[n + 2], 0, 3)
    for d in (2, 1, 3):
        for h in range(2):
            arrive(fin1.at[h, d], f1[h, d])
            s1[h, d] = (
                pp[walker(h, 0, d)].astype(F32) + fin1[h, d, 0].astype(F32) + fin1[h, d, 1].astype(F32)
            ).astype(BF16)
            send(s1.at[h, d], last.at[core * 5 + 1 + d], dev(chip_of(h, 0, d), h), fl)

    arrive(ebuf.at[1, pl.ds(1, 3)], ey)
    ebuf[1, 0] = esend[1]
    row = ordered_sum(ebuf, 1, py)
    e_ref[...] = row[0:1, 0:32]

    mine = 2 * chip + core
    arrive(last, fl)
    for o in range(2):
        own = jnp.where(core == o, pp[mine].astype(F32), last[10].astype(F32))
        for n in range(5):
            own = own + last[o * 5 + n].astype(F32)
        full = step_factor * own
        near, far = full[:, :128], full[:, 128:]
        near = jnp.concatenate([near[:BLOCK], pltpu.roll(near[BLOCK:], BLOCK, 1)], axis=0)
        pair = [near, far] if o == 0 else [far, near]
        pot[o * 128:(o + 1) * 128, :] = jnp.concatenate(pair, axis=1).astype(BF16)
    arrive(tbuf.at[other], wi)
    start = tbuf[...].reshape(NORB, NOCC)
    term = start
    total = jnp.zeros((NORB, NOCC), F32)
    for degree in range(1, TAYLOR + 1):
        product = jnp.dot(pot[...], term, preferred_element_type=F32)
        term = (product / degree).astype(BF16)
        total = total + term.astype(F32)
    nw[...] = (start.astype(F32) + total).astype(BF16).reshape(2, 128, NOCC)

    g1 = slots(6)
    g2 = slots()
    for d in (2, 1, 3):
        for o in range(2):
            send(nw.at[o], out.at[mine], dev(chip_at(core * d, other * d), o), g1 + core * 3 + d - 1)
    for d in (2, 1, 3):
        for o in range(2):
            send(nw.at[o], out.at[mine], dev(chip_at(other * d, core * d), o), g2)
    send(nw.at[other], out.at[mine], dev(chip, other), g2)
    keep = pltpu.make_async_copy(nw.at[core], out.at[mine], lsem.at[0])
    keep.start()
    for d in (1, 3, 2):
        for h in range(2):
            w = walker(h, 0, 4 - d)
            arrive(out.at[w], g1 + h * 3 + d - 1)
            for da in (2, 1, 3):
                send(out.at[w], out.at[w], dev(chip_of(h, da, 0), core), g2)
    keep.wait()
    arrive(out.at[pl.ds(0, 25)], g2)
    whole = pl.ds(0, 190)
    pltpu.make_async_copy(vbuf.at[pl.ds(0, 4), whole], vbuf.at[pl.ds(4, 4), whole], ssem.at[0]).wait()
    pltpu.make_async_copy(ebuf.at[:, pl.ds(0, 3)], ebuf.at[:, pl.ds(1, 3)], ssem.at[1]).wait()
    assert used[0] == SEMS, used[0]


def ordered_sum(ebuf, stage, at):
    rows = [ebuf[stage, (at - q + SIDE) % SIDE] for q in range(SIDE)]
    return (rows[0] + rows[1]) + (rows[2] + rows[3])


SEMS = 34


def per_device(chol_vals, chol_cols, greens, walkers, fields):
    vectors = chol_vals.shape[0]
    step_factor = 72.0 / float(vectors * lax.axis_size("chol") * BLOCK) ** 0.5
    vmem = pltpu.VMEM
    hbm = pl.BlockSpec(memory_space=pltpu.HBM)
    new_walkers, energy = pl.pallas_call(
        functools.partial(kernel, step_factor),
        out_shape=(
            jax.ShapeDtypeStruct((32, 128, NOCC), BF16),
            jax.ShapeDtypeStruct((1, 32), F32),
        ),
        in_specs=[hbm] * 5,
        out_specs=(pl.BlockSpec(memory_space=pl.ANY), pl.BlockSpec(memory_space=vmem)),
        scratch_shapes=[
            vmem((8, 256, 16, 128), BF16),
            vmem((2, 256, 64 * 128), BF16),
            vmem((32, 128, 256), BF16),
            vmem((2, 128, 64 * 128), BF16),
            vmem((2, 2, 256), jnp.int32),
            vmem((32, 256), F32),
            vmem((2, 128, NOCC), BF16),
            vmem((2, 128, NOCC), BF16),
            vmem((32, 256), F32),
            vmem((32, 256), F32),
            vmem((32, 128, 256), BF16),
            vmem((2, 4, 2, HALF, 256), BF16),
            vmem((2, 4, 2, 128, 256), BF16),
            vmem((2, 4, 128, 256), BF16),
            vmem((11, 128, 256), BF16),
            vmem((NORB, NORB), BF16),
            vmem((2, 128, NOCC), BF16),
            vmem((2, 8, 128), F32),
            vmem((2, SIDE, 8, 128), F32),
            pltpu.SemaphoreType.DMA((19,)),
            pltpu.SemaphoreType.DMA((2,)),
            pltpu.SemaphoreType.DMA((SEMS,)),
        ],
        compiler_params=pltpu.CompilerParams(
            collective_id=0, has_side_effects=True, vmem_limit_bytes=44 << 20
        ),
    )(*[pltpu.with_memory_space_constraint(a, pltpu.HBM) for a in (chol_vals, chol_cols.transpose(1, 2, 0), greens, walkers, fields.T)])
    return new_walkers, energy.reshape(32)


def solution(mesh):
    in_specs = (
        P("chol", "orb", None, None),
        P("chol", "orb", None),
        P("walker", "orb", None),
        P("walker", "orb", None),
        P("chol", "walker"),
    )
    out_specs = (P("walker", "orb", None), P("walker"))
    return jax.shard_map(
        per_device, mesh=mesh, in_specs=in_specs, out_specs=out_specs, check_vma=False
    )
```

```python
import functools

import jax
import jax.numpy as jnp
from jax import lax
from jax.experimental import pallas as pl
from jax.experimental.pallas import tpu as pltpu
from jax.sharding import PartitionSpec as P

NORB = 256
NOCC = 128
BLOCK = 64
TAYLOR = 4
SIDE = 4
F32 = jnp.float32
BF16 = jnp.bfloat16
MESH = pl.DeviceIdType.MESH
HALF = 64
WAY = (1, 3)


def swap_halves(x):
    return jnp.concatenate([x[:, BLOCK:], x[:, :BLOCK]], axis=1)


def kernel(
    step_factor, v_hbm, cols_hbm, g_hbm, w_hbm, f_hbm, out, e_ref,
    vbuf, vt, gbuf, gp, cbuf, fbuf, wbuf, tbuf, fx, fxr,
    pp, opp1, fin1, s1, last, pot, nw, esend, ebuf,
    lsem, ssem, rsem,
):
    chip = lax.axis_index("chol")
    core = lax.axis_index("orb")
    other = 1 - core
    px, py = chip // SIDE, chip % SIDE

    def chip_at(dx, dy):
        return ((px + dx) % SIDE) * SIDE + (py + dy) % SIDE

    def chip_of(h, da, db):
        return chip_at(da, db) if h == 0 else chip_at(db, da)

    def walker(h, da, db):
        return 2 * chip_of(h, da, db) + h

    def dev(c, k):
        return {"chol": c, "orb": k}

    used = [0]

    def slots(n=1):
        used[0] += n
        return used[0] - n

    def remote(src, dst, to, ridx, small=0):
        return pltpu.make_async_remote_copy(
            src_ref=src, dst_ref=dst, send_sem=ssem.at[small], recv_sem=rsem.at[ridx],
            device_id=to, device_id_type=MESH,
        )

    def send(src, dst, to, ridx, small=0):
        remote(src, dst, to, ridx, small).start()

    def arrive(dst, ridx):
        remote(dst, dst, dev(chip, other), ridx).wait_recv()

    barrier = pltpu.get_barrier_semaphore()
    partners = [dev(chip, other)]
    for dx, dy in ((1, 0), (3, 0), (2, 0), (0, 1), (0, 3), (0, 2)):
        partners += [dev(chip_at(dx, dy), core), dev(chip_at(dx, dy), other)]
    for to in partners:
        pl.semaphore_signal(barrier, inc=1, device_id=to, device_id_type=MESH)

    def load_g(n):
        rows = pl.ds(n * 16, 16)
        return pltpu.make_async_copy(g_hbm.at[:, rows, :], gbuf.at[:, rows, :], lsem.at[8 + n])

    def load_v(r, ii):
        n = r * 4 + ii
        return pltpu.make_async_copy(v_hbm.at[:, r, pl.ds(ii * 16, 16), :], vbuf.at[n], lsem.at[n])

    for r in range(2):
        for ii in range(4):
            load_g(r * 4 + ii).start()
            load_v(r, ii).start()
    fcopy = pltpu.make_async_copy(f_hbm, fbuf, lsem.at[16])
    fcopy.start()
    ccopy = pltpu.make_async_copy(cols_hbm, cbuf, lsem.at[17])
    ccopy.start()
    wcopy = pltpu.make_async_copy(w_hbm.at[pl.ds(2 * chip, 2)], wbuf, lsem.at[18])
    wcopy.start()

    low = lax.broadcasted_iota(jnp.int32, (16, 128), 1) < BLOCK
    own_at = pl.multiple_of(core * 128, 128)
    far_at = pl.multiple_of(other * 128, 128)
    for r in range(2):

        @pl.loop(0, 4)
        def _(ii):
            load_g(r * 4 + ii).wait()
            load_v(r, ii).wait()
            rows = pl.ds(pl.multiple_of(r * 64 + ii * 16, 16), 16)
            k0 = pl.multiple_of(ii * 2048, 2048)
            for w0 in (0, 16):
                near = jnp.swapaxes(gbuf[w0:w0 + 16, rows, pl.ds(own_at, 128)], 0, 1)
                far = jnp.swapaxes(gbuf[w0:w0 + 16, rows, pl.ds(far_at, 128)], 0, 1)
                for i in range(16):
                    a, b = near[i], far[i]
                    if r == 1:
                        a = swap_halves(a)
                    z = jnp.zeros_like(a)
                    choices = (jnp.where(low, a, z), a, jnp.where(low, a, swap_halves(b)), jnp.where(low, a, b))
                    for c, val in enumerate(choices):
                        gp[r, c * 32 + w0:c * 32 + w0 + 16, pl.ds(k0 + i * 128, 128)] = val
            for g0 in range(0, 256, 16):
                y = jnp.swapaxes(vbuf[r * 4 + ii, g0:g0 + 16, :, :], 0, 1)
                for i in range(16):
                    vt[r, g0:g0 + 16, pl.ds(k0 + i * 128, 128)] = y[i]

    fcopy.wait()
    ccopy.wait()
    wcopy.wait()
    masks = []
    partial = jnp.zeros((32, 256), F32)
    for r in range(2):
        acc = lax.dot_general(vt[r], gp[r], (((1,), (1,)), ((), ())), preferred_element_type=F32).T
        code = cbuf[r, 1:2, :]
        wanted = (4, 2 * core + (1 - r), 2 * other, 2 * other + 1)
        ms = [code == k for k in wanted]
        masks.append(ms)
        for c in range(4):
            partial = partial + jnp.where(ms[c], acc[c * 32:(c + 1) * 32], 0.0)
    fx[...] = partial
    tbuf[core] = wbuf[core]
    fi, wi = slots(), slots()
    pl.semaphore_wait(barrier, len(partners))
    send(fx, fxr, dev(chip, other), fi)
    send(wbuf.at[other], tbuf.at[core], dev(chip, other), wi)
    arrive(fxr, fi)
    bias = partial + fxr[...]
    shifted = fbuf[...] - bias

    local = 0.5 * jnp.sum(bias * bias, axis=1, keepdims=True)
    diag = lax.broadcasted_iota(jnp.int32, (32, 128), 0) == lax.broadcasted_iota(jnp.int32, (32, 128), 1)
    row = jnp.sum(jnp.where(diag, local, 0.0), axis=0, keepdims=True)
    esend[0] = jnp.broadcast_to(row, (8, 128))
    ex, ey = slots(), slots()
    for d in (1, 2, 3):
        send(esend.at[0], ebuf.at[0, d], dev(chip_at(d, 0), core), ex, 1)

    lo32 = lax.broadcasted_iota(jnp.int32, (32, 128), 1) < BLOCK
    order = (2, 1, 3, 0)
    o1 = {(h, d, r): slots() for h in range(2) for d in range(4) for r in range(2)}
    f1 = {(h, d): slots() for h in range(2) for d in (1, 2, 3)}
    fl = slots()

    def rows_of(r, q):
        return pl.ds(r * HALF + q * 32, 32)

    def send_opp(d, r, q):
        for h in range(2):
            src = pp.at[walker(h, 2, d), rows_of(r, q)]
            send(src, opp1.at[h, d, r, q], dev(chip_of(h, WAY[q], 0), core), o1[h, d, r])

    def send_target(d, r, q, s):
        for h in range(2):
            src = pp.at[walker(h, WAY[s], d), rows_of(r, q)]
            if d == 0:
                send(src, last.at[core * 5 + s, rows_of(r, q)], dev(chip_of(h, WAY[s], 0), h), fl)
            else:
                send(src, fin1.at[h, d, s, rows_of(r, q)], dev(chip_of(h, WAY[s], 0), core), f1[h, d])

    def send_own(d, r):
        for s in range(2):
            send_target(d, r, 1 - s, s)

    def add_opp(d, r):
        for h in range(2):
            arrive(opp1.at[h, d, r], o1[h, d, r])
            for q in range(2):
                w = walker(h, WAY[q], d)
                pp[w, rows_of(r, q)] = (pp[w, rows_of(r, q)].astype(F32) + opp1[h, d, r, q].astype(F32)).astype(BF16)
        for s in range(2):
            send_target(d, r, s, s)

    for r in range(2):
        parts = [shifted] + [jnp.where(masks[r][c], shifted, 0.0) for c in (1, 2, 3)]
        lhs = jnp.concatenate(parts, axis=0).astype(BF16)

        def part(ii):
            k0 = pl.multiple_of(ii * 2048, 2048)
            o = jnp.dot(lhs, vt[r, :, pl.ds(k0, 2048)], preferred_element_type=F32)
            x0, x1 = [], []
            for i in range(16):
                t = o[:, i * 128:(i + 1) * 128]
                x0.append(jnp.where(lo32, t[0:32], t[32:64]).astype(BF16))
                x1.append(jnp.where(lo32, pltpu.roll(t[64:96], 64, 1), t[96:128]).astype(BF16))
            i0 = pl.multiple_of(r * 64 + ii * 16, 16)
            for wh in range(2):
                for side, x in ((0, x0), (1, x1)):
                    s = jnp.stack([q[wh * 16:(wh + 1) * 16] for q in x], axis=0)
                    pp[wh * 16:(wh + 1) * 16, pl.ds(i0, 16), side * 128:(side + 1) * 128] = jnp.swapaxes(s, 0, 1)

        for q in range(2):
            pl.loop(2 * q, 2 * q + 2)(part)
            for d in order:
                send_opp(d, r, q)
        if r == 0:
            send_own(2, 0)
            send_own(1, 0)
    send(pp.at[2 * chip + other], last.at[10], dev(chip, other), fl)

    arrive(ebuf.at[0, pl.ds(1, 3)], ex)
    ebuf[0, 0] = esend[0]
    row = ordered_sum(ebuf, 0, px)
    esend[1] = row
    for d in (1, 2, 3):
        send(esend.at[1], ebuf.at[1, d], dev(chip_at(0, d), core), ey, 1)

    send_own(2, 1)
    add_opp(2, 0)
    add_opp(1, 0)
    send_own(1, 1)
    add_opp(2, 1)
    add_opp(1, 1)
    for d in (3, 0):
        for r in range(2):
            send_own(d, r)
        for r in range(2):
            add_opp(d, r)
    for d in (2, 1, 3):
        for h in range(2):
            arrive(fin1.at[h, d], f1[h, d])
            s1[h, d] = (
                pp[walker(h, 0, d)].astype(F32) + fin1[h, d, 0].astype(F32) + fin1[h, d, 1].astype(F32)
            ).astype(BF16)
            send(s1.at[h, d], last.at[core * 5 + 1 + d], dev(chip_of(h, 0, d), h), fl)

    arrive(ebuf.at[1, pl.ds(1, 3)], ey)
    ebuf[1, 0] = esend[1]
    row = ordered_sum(ebuf, 1, py)
    e_ref[...] = row[0:1, 0:32]

    mine = 2 * chip + core
    arrive(last, fl)
    for o in range(2):
        own = jnp.where(core == o, pp[mine].astype(F32), last[10].astype(F32))
        for n in range(5):
            own = own + last[o * 5 + n].astype(F32)
        full = step_factor * own
        near, far = full[:, :128], full[:, 128:]
        near = jnp.concatenate([near[:BLOCK], pltpu.roll(near[BLOCK:], BLOCK, 1)], axis=0)
        pair = [near, far] if o == 0 else [far, near]
        pot[o * 128:(o + 1) * 128, :] = jnp.concatenate(pair, axis=1).astype(BF16)
    arrive(tbuf.at[other], wi)
    start = tbuf[...].reshape(NORB, NOCC)
    term = start
    total = jnp.zeros((NORB, NOCC), F32)
    for degree in range(1, TAYLOR + 1):
        product = jnp.dot(pot[...], term, preferred_element_type=F32)
        term = (product / degree).astype(BF16)
        total = total + term.astype(F32)
    nw[...] = (start.astype(F32) + total).astype(BF16).reshape(2, 128, NOCC)

    g1 = slots(6)
    g2 = slots()
    for d in (2, 1, 3):
        for o in range(2):
            send(nw.at[o], out.at[mine], dev(chip_at(core * d, other * d), o), g1 + core * 3 + d - 1, 2)
    send(nw.at[other], out.at[mine], dev(chip, other), g2)
    keep = pltpu.make_async_copy(nw.at[core], out.at[mine], lsem.at[0])
    keep.start()
    sent_first = pl.ds(0, 48)
    pltpu.make_async_copy(vbuf.at[0, sent_first], vbuf.at[1, sent_first], ssem.at[2]).wait()
    for d in (2, 1, 3):
        for o in range(2):
            send(nw.at[o], out.at[mine], dev(chip_at(other * d, core * d), o), g2)
    for d in (1, 3, 2):
        for h in range(2):
            w = walker(h, 0, 4 - d)
            arrive(out.at[w], g1 + h * 3 + d - 1)
            for da in (2, 1, 3):
                send(out.at[w], out.at[w], dev(chip_of(h, da, 0), core), g2)
    keep.wait()
    arrive(out.at[pl.ds(0, 25)], g2)
    whole = pl.ds(0, 178)
    pltpu.make_async_copy(vbuf.at[pl.ds(0, 4), whole], vbuf.at[pl.ds(4, 4), whole], ssem.at[0]).wait()
    pltpu.make_async_copy(ebuf.at[:, pl.ds(0, 3)], ebuf.at[:, pl.ds(1, 3)], ssem.at[1]).wait()
    assert used[0] == SEMS, used[0]


def ordered_sum(ebuf, stage, at):
    rows = [ebuf[stage, (at - q + SIDE) % SIDE] for q in range(SIDE)]
    return (rows[0] + rows[1]) + (rows[2] + rows[3])


SEMS = 34


def write_out(w_ref, e_ref, w_out, e_out, sem):
    copies = [
        pltpu.make_async_copy(w_ref, w_out, sem.at[0]),
        pltpu.make_async_copy(e_ref, e_out, sem.at[1]),
    ]
    for c in copies:
        c.start()
    for c in copies:
        c.wait()


def per_device(chol_vals, chol_cols, greens, walkers, fields):
    vectors = chol_vals.shape[0]
    step_factor = 72.0 / float(vectors * lax.axis_size("chol") * BLOCK) ** 0.5
    vmem = pltpu.VMEM
    hbm = pl.BlockSpec(memory_space=pltpu.HBM)
    new_walkers, energy = pl.pallas_call(
        functools.partial(kernel, step_factor),
        out_shape=(
            jax.ShapeDtypeStruct((32, 128, NOCC), BF16),
            jax.ShapeDtypeStruct((1, 32), F32),
        ),
        in_specs=[hbm] * 5,
        out_specs=(pl.BlockSpec(memory_space=pl.ANY), pl.BlockSpec(memory_space=vmem)),
        scratch_shapes=[
            vmem((8, 256, 16, 128), BF16),
            vmem((2, 256, 64 * 128), BF16),
            vmem((32, 128, 256), BF16),
            vmem((2, 128, 64 * 128), BF16),
            vmem((2, 2, 256), jnp.int32),
            vmem((32, 256), F32),
            vmem((2, 128, NOCC), BF16),
            vmem((2, 128, NOCC), BF16),
            vmem((32, 256), F32),
            vmem((32, 256), F32),
            vmem((32, 128, 256), BF16),
            vmem((2, 4, 2, 2, 32, 256), BF16),
            vmem((2, 4, 2, 128, 256), BF16),
            vmem((2, 4, 128, 256), BF16),
            vmem((11, 128, 256), BF16),
            vmem((NORB, NORB), BF16),
            vmem((2, 128, NOCC), BF16),
            vmem((2, 8, 128), F32),
            vmem((2, SIDE, 8, 128), F32),
            pltpu.SemaphoreType.DMA((19,)),
            pltpu.SemaphoreType.DMA((3,)),
            pltpu.SemaphoreType.DMA((SEMS,)),
        ],
        compiler_params=pltpu.CompilerParams(
            collective_id=0, has_side_effects=True, vmem_limit_bytes=44 << 20
        ),
    )(*[pltpu.with_memory_space_constraint(a, pltpu.HBM) for a in (chol_vals, chol_cols.transpose(1, 2, 0), greens, walkers, fields.T)])
    in_vmem = pl.BlockSpec(memory_space=pl.ANY)
    new_walkers, energy = pl.pallas_call(
        write_out,
        out_shape=(
            jax.ShapeDtypeStruct((32, 128, NOCC), BF16),
            jax.ShapeDtypeStruct((1, 32), F32),
        ),
        in_specs=[in_vmem, in_vmem],
        out_specs=(hbm, hbm),
        scratch_shapes=[pltpu.SemaphoreType.DMA((2,))],
        compiler_params=pltpu.CompilerParams(vmem_limit_bytes=8 << 20),
    )(new_walkers, energy)
    return new_walkers, energy.reshape(32)


def solution(mesh):
    in_specs = (
        P("chol", "orb", None, None),
        P("chol", "orb", None),
        P("walker", "orb", None),
        P("walker", "orb", None),
        P("chol", "walker"),
    )
    out_specs = (P("walker", "orb", None), P("walker"))
    return jax.shard_map(
        per_device, mesh=mesh, in_specs=in_specs, out_specs=out_specs, check_vma=False
    )
```

```python
import functools

import jax
import jax.numpy as jnp
from jax import lax
from jax.experimental import pallas as pl
from jax.experimental.pallas import tpu as pltpu
from jax.sharding import PartitionSpec as P

NORB = 256
NOCC = 128
BLOCK = 64
TAYLOR = 4
SIDE = 4
F32 = jnp.float32
BF16 = jnp.bfloat16
MESH = pl.DeviceIdType.MESH
HALF = 64
WAY = (1, 3)


def swap_halves(x):
    return jnp.concatenate([x[:, BLOCK:], x[:, :BLOCK]], axis=1)


def kernel(
    step_factor, v_hbm, cols_hbm, g_hbm, w_hbm, f_hbm, out, e_ref,
    vbuf, vt, gbuf, gp, cbuf, fbuf, wbuf, tbuf, fx, fxr,
    pp, opp1, fin1, s1, last, pot, nw, esend, ebuf,
    lsem, ssem, rsem,
):
    chip = lax.axis_index("chol")
    core = lax.axis_index("orb")
    other = 1 - core
    px, py = chip // SIDE, chip % SIDE

    def chip_at(dx, dy):
        return ((px + dx) % SIDE) * SIDE + (py + dy) % SIDE

    def chip_of(h, da, db):
        return chip_at(da, db) if h == 0 else chip_at(db, da)

    def walker(h, da, db):
        return 2 * chip_of(h, da, db) + h

    def dev(c, k):
        return {"chol": c, "orb": k}

    used = [0]

    def slots(n=1):
        used[0] += n
        return used[0] - n

    def remote(src, dst, to, ridx, small=0):
        return pltpu.make_async_remote_copy(
            src_ref=src, dst_ref=dst, send_sem=ssem.at[small], recv_sem=rsem.at[ridx],
            device_id=to, device_id_type=MESH,
        )

    def send(src, dst, to, ridx, small=0):
        remote(src, dst, to, ridx, small).start()

    def arrive(dst, ridx):
        remote(dst, dst, dev(chip, other), ridx).wait_recv()

    barrier = pltpu.get_barrier_semaphore()
    partners = [dev(chip, other)]
    for dx, dy in ((1, 0), (3, 0), (2, 0), (0, 1), (0, 3), (0, 2)):
        partners += [dev(chip_at(dx, dy), core), dev(chip_at(dx, dy), other)]
    for to in partners:
        pl.semaphore_signal(barrier, inc=1, device_id=to, device_id_type=MESH)

    def load_g(n):
        rows = pl.ds(n * 16, 16)
        return pltpu.make_async_copy(g_hbm.at[:, rows, :], gbuf.at[:, rows, :], lsem.at[8 + n])

    def load_v(r, ii):
        n = r * 4 + ii
        return pltpu.make_async_copy(v_hbm.at[:, r, pl.ds(ii * 16, 16), :], vbuf.at[n], lsem.at[n])

    for r in range(2):
        for ii in range(4):
            load_g(r * 4 + ii).start()
            load_v(r, ii).start()
    fcopy = pltpu.make_async_copy(f_hbm, fbuf, lsem.at[16])
    fcopy.start()
    ccopy = pltpu.make_async_copy(cols_hbm, cbuf, lsem.at[17])
    ccopy.start()
    wcopy = pltpu.make_async_copy(w_hbm.at[pl.ds(2 * chip, 2)], wbuf, lsem.at[18])
    wcopy.start()

    low = lax.broadcasted_iota(jnp.int32, (16, 128), 1) < BLOCK
    own_at = pl.multiple_of(core * 128, 128)
    far_at = pl.multiple_of(other * 128, 128)
    for r in range(2):

        @pl.loop(0, 4)
        def _(ii):
            load_g(r * 4 + ii).wait()
            load_v(r, ii).wait()
            rows = pl.ds(pl.multiple_of(r * 64 + ii * 16, 16), 16)
            k0 = pl.multiple_of(ii * 2048, 2048)
            for w0 in (0, 16):
                near = jnp.swapaxes(gbuf[w0:w0 + 16, rows, pl.ds(own_at, 128)], 0, 1)
                far = jnp.swapaxes(gbuf[w0:w0 + 16, rows, pl.ds(far_at, 128)], 0, 1)
                for i in range(16):
                    a, b = near[i], far[i]
                    if r == 1:
                        a = swap_halves(a)
                    z = jnp.zeros_like(a)
                    choices = (jnp.where(low, a, z), a, jnp.where(low, a, swap_halves(b)), jnp.where(low, a, b))
                    for c, val in enumerate(choices):
                        gp[r, c * 32 + w0:c * 32 + w0 + 16, pl.ds(k0 + i * 128, 128)] = val
            for g0 in range(0, 256, 16):
                y = jnp.swapaxes(vbuf[r * 4 + ii, g0:g0 + 16, :, :], 0, 1)
                for i in range(16):
                    vt[r, g0:g0 + 16, pl.ds(k0 + i * 128, 128)] = y[i]

    fcopy.wait()
    ccopy.wait()
    wcopy.wait()
    masks = []
    partial = jnp.zeros((32, 256), F32)
    for r in range(2):
        acc = lax.dot_general(vt[r], gp[r], (((1,), (1,)), ((), ())), preferred_element_type=F32).T
        code = cbuf[r, 1:2, :]
        wanted = (4, 2 * core + (1 - r), 2 * other, 2 * other + 1)
        ms = [code == k for k in wanted]
        masks.append(ms)
        for c in range(4):
            partial = partial + jnp.where(ms[c], acc[c * 32:(c + 1) * 32], 0.0)
    fx[...] = partial
    tbuf[core] = wbuf[core]
    fi, wi = slots(), slots()
    pl.semaphore_wait(barrier, len(partners))
    send(fx, fxr, dev(chip, other), fi)
    send(wbuf.at[other], tbuf.at[core], dev(chip, other), wi)
    arrive(fxr, fi)
    bias = partial + fxr[...]
    shifted = fbuf[...] - bias

    local = 0.5 * jnp.sum(bias * bias, axis=1, keepdims=True)
    diag = lax.broadcasted_iota(jnp.int32, (32, 128), 0) == lax.broadcasted_iota(jnp.int32, (32, 128), 1)
    row = jnp.sum(jnp.where(diag, local, 0.0), axis=0, keepdims=True)
    esend[0] = jnp.broadcast_to(row, (8, 128))
    ex, ey = slots(), slots()
    for d in (1, 2, 3):
        send(esend.at[0], ebuf.at[0, d], dev(chip_at(d, 0), core), ex, 1)

    lo32 = lax.broadcasted_iota(jnp.int32, (32, 128), 1) < BLOCK
    o1 = {(h, d, r): slots() for h in range(2) for d in range(4) for r in range(2)}
    f1 = {(h, d, r): slots() for h in range(2) for d in (1, 2, 3) for r in range(2)}
    fl = slots()

    def rows_of(r, q):
        return pl.ds(r * HALF + q * 32, 32)

    def send_opp(d, r, q):
        for h in range(2):
            src = pp.at[walker(h, 2, d), rows_of(r, q)]
            send(src, opp1.at[h, d, r, q], dev(chip_of(h, WAY[q], 0), core), o1[h, d, r])

    def send_target(d, r, q, s):
        for h in range(2):
            src = pp.at[walker(h, WAY[s], d), rows_of(r, q)]
            if d == 0:
                send(src, last.at[core * 5 + s, rows_of(r, q)], dev(chip_of(h, WAY[s], 0), h), fl)
            else:
                send(src, fin1.at[h, d, r, s, q], dev(chip_of(h, WAY[s], 0), core), f1[h, d, r])

    def send_own(d, r):
        for s in range(2):
            send_target(d, r, 1 - s, s)

    def add_opp(d, r):
        for h in range(2):
            arrive(opp1.at[h, d, r], o1[h, d, r])
            for q in range(2):
                w = walker(h, WAY[q], d)
                pp[w, rows_of(r, q)] = (pp[w, rows_of(r, q)].astype(F32) + opp1[h, d, r, q].astype(F32)).astype(BF16)
        for s in range(2):
            send_target(d, r, s, s)

    for r in range(2):
        parts = [shifted] + [jnp.where(masks[r][c], shifted, 0.0) for c in (1, 2, 3)]
        lhs = jnp.concatenate(parts, axis=0).astype(BF16)

        def part(ii):
            k0 = pl.multiple_of(ii * 2048, 2048)
            o = jnp.dot(lhs, vt[r, :, pl.ds(k0, 2048)], preferred_element_type=F32)
            x0, x1 = [], []
            for i in range(16):
                t = o[:, i * 128:(i + 1) * 128]
                x0.append(jnp.where(lo32, t[0:32], t[32:64]).astype(BF16))
                x1.append(jnp.where(lo32, pltpu.roll(t[64:96], 64, 1), t[96:128]).astype(BF16))
            i0 = pl.multiple_of(r * 64 + ii * 16, 16)
            for wh in range(2):
                for side, x in ((0, x0), (1, x1)):
                    s = jnp.stack([q[wh * 16:(wh + 1) * 16] for q in x], axis=0)
                    pp[wh * 16:(wh + 1) * 16, pl.ds(i0, 16), side * 128:(side + 1) * 128] = jnp.swapaxes(s, 0, 1)

        for q in range(2):
            pl.loop(2 * q, 2 * q + 2)(part)
            for d in (2, 1, 3) if r else (2, 1, 3, 0):
                send_opp(d, r, q)
        for d in (2, 1) if r else (2, 1, 3, 0):
            send_own(d, r)
    send(pp.at[2 * chip + other], last.at[10], dev(chip, other), fl)

    arrive(ebuf.at[0, pl.ds(1, 3)], ex)
    ebuf[0, 0] = esend[0]
    row = ordered_sum(ebuf, 0, px)
    esend[1] = row
    for d in (1, 2, 3):
        send(esend.at[1], ebuf.at[1, d], dev(chip_at(0, d), core), ey, 1)

    def finish(d, r):
        rows = pl.ds(r * HALF, HALF)
        for h in range(2):
            arrive(fin1.at[h, d, r], f1[h, d, r])
            both = fin1[h, d, r, 0].astype(F32) + fin1[h, d, r, 1].astype(F32)
            s1[h, d, r] = (pp[walker(h, 0, d), rows].astype(F32) + both.reshape(HALF, 256)).astype(BF16)
            send(s1.at[h, d, r], last.at[core * 5 + 1 + d, rows], dev(chip_of(h, 0, d), h), fl)

    for d in (2, 1, 3):
        add_opp(d, 0)
    send_own(3, 1)
    add_opp(0, 0)
    for q in range(2):
        send_opp(0, 1, q)
    send_own(0, 1)
    for d in (2, 1, 3):
        add_opp(d, 1)
    for d in (2, 1, 3):
        finish(d, 0)
    add_opp(0, 1)
    for d in (2, 1, 3):
        finish(d, 1)

    arrive(ebuf.at[1, pl.ds(1, 3)], ey)
    ebuf[1, 0] = esend[1]
    row = ordered_sum(ebuf, 1, py)
    e_ref[...] = row[0:1, 0:32]

    mine = 2 * chip + core
    arrive(last, fl)
    for o in range(2):
        own = jnp.where(core == o, pp[mine].astype(F32), last[10].astype(F32))
        for n in range(5):
            own = own + last[o * 5 + n].astype(F32)
        full = step_factor * own
        near, far = full[:, :128], full[:, 128:]
        near = jnp.concatenate([near[:BLOCK], pltpu.roll(near[BLOCK:], BLOCK, 1)], axis=0)
        pair = [near, far] if o == 0 else [far, near]
        pot[o * 128:(o + 1) * 128, :] = jnp.concatenate(pair, axis=1).astype(BF16)
    arrive(tbuf.at[other], wi)
    start = tbuf[...].reshape(NORB, NOCC)
    term = start
    total = jnp.zeros((NORB, NOCC), F32)
    for degree in range(1, TAYLOR + 1):
        product = jnp.dot(pot[...], term, preferred_element_type=F32)
        term = (product / degree).astype(BF16)
        total = total + term.astype(F32)
    nw[...] = (start.astype(F32) + total).astype(BF16).reshape(2, 128, NOCC)

    g1 = slots(6)
    g2 = slots()
    for d in (1, 3, 2):
        for o in range(2):
            to = dev(chip_at(core * d, other * d), o)
            send(nw.at[o], out.at[mine], to, g1 + core * 3 + d - 1, 0 if d == 2 else 2)
    send(nw.at[other], out.at[mine], dev(chip, other), g2)
    keep = pltpu.make_async_copy(nw.at[core], out.at[mine], lsem.at[0])
    keep.start()
    sent_first = pl.ds(0, 32)
    pltpu.make_async_copy(vbuf.at[0, sent_first], vbuf.at[1, sent_first], ssem.at[2]).wait()
    for d in (2, 1, 3):
        for o in range(2):
            send(nw.at[o], out.at[mine], dev(chip_at(other * d, core * d), o), g2)
    for d in (1, 3, 2):
        for h in range(2):
            w = walker(h, 0, 4 - d)
            arrive(out.at[w], g1 + h * 3 + d - 1)
            for da in (2, 1, 3):
                send(out.at[w], out.at[w], dev(chip_of(h, da, 0), core), g2)
    keep.wait()
    arrive(out.at[pl.ds(0, 25)], g2)
    whole = pl.ds(0, 182)
    pltpu.make_async_copy(vbuf.at[pl.ds(0, 4), whole], vbuf.at[pl.ds(4, 4), whole], ssem.at[0]).wait()
    pltpu.make_async_copy(ebuf.at[:, pl.ds(0, 3)], ebuf.at[:, pl.ds(1, 3)], ssem.at[1]).wait()
    assert used[0] == SEMS, used[0]


def ordered_sum(ebuf, stage, at):
    rows = [ebuf[stage, (at - q + SIDE) % SIDE] for q in range(SIDE)]
    return (rows[0] + rows[1]) + (rows[2] + rows[3])


SEMS = 40


def write_out(w_ref, e_ref, w_out, e_out, sem):
    copies = [
        pltpu.make_async_copy(w_ref, w_out, sem.at[0]),
        pltpu.make_async_copy(e_ref, e_out, sem.at[1]),
    ]
    for c in copies:
        c.start()
    for c in copies:
        c.wait()


def per_device(chol_vals, chol_cols, greens, walkers, fields):
    vectors = chol_vals.shape[0]
    step_factor = 72.0 / float(vectors * lax.axis_size("chol") * BLOCK) ** 0.5
    vmem = pltpu.VMEM
    hbm = pl.BlockSpec(memory_space=pltpu.HBM)
    new_walkers, energy = pl.pallas_call(
        functools.partial(kernel, step_factor),
        out_shape=(
            jax.ShapeDtypeStruct((32, 128, NOCC), BF16),
            jax.ShapeDtypeStruct((1, 32), F32),
        ),
        in_specs=[hbm] * 5,
        out_specs=(pl.BlockSpec(memory_space=pl.ANY), pl.BlockSpec(memory_space=vmem)),
        scratch_shapes=[
            vmem((8, 256, 16, 128), BF16),
            vmem((2, 256, 64 * 128), BF16),
            vmem((32, 128, 256), BF16),
            vmem((2, 128, 64 * 128), BF16),
            vmem((2, 2, 256), jnp.int32),
            vmem((32, 256), F32),
            vmem((2, 128, NOCC), BF16),
            vmem((2, 128, NOCC), BF16),
            vmem((32, 256), F32),
            vmem((32, 256), F32),
            vmem((32, 128, 256), BF16),
            vmem((2, 4, 2, 2, 32, 256), BF16),
            vmem((2, 4, 2, 2, 2, 32, 256), BF16),
            vmem((2, 4, 2, HALF, 256), BF16),
            vmem((11, 128, 256), BF16),
            vmem((NORB, NORB), BF16),
            vmem((2, 128, NOCC), BF16),
            vmem((2, 8, 128), F32),
            vmem((2, SIDE, 8, 128), F32),
            pltpu.SemaphoreType.DMA((19,)),
            pltpu.SemaphoreType.DMA((3,)),
            pltpu.SemaphoreType.DMA((SEMS,)),
        ],
        compiler_params=pltpu.CompilerParams(
            collective_id=0, has_side_effects=True, vmem_limit_bytes=44 << 20
        ),
    )(*[pltpu.with_memory_space_constraint(a, pltpu.HBM) for a in (chol_vals, chol_cols.transpose(1, 2, 0), greens, walkers, fields.T)])
    in_vmem = pl.BlockSpec(memory_space=pl.ANY)
    new_walkers, energy = pl.pallas_call(
        write_out,
        out_shape=(
            jax.ShapeDtypeStruct((32, 128, NOCC), BF16),
            jax.ShapeDtypeStruct((1, 32), F32),
        ),
        in_specs=[in_vmem, in_vmem],
        out_specs=(hbm, hbm),
        scratch_shapes=[pltpu.SemaphoreType.DMA((2,))],
        compiler_params=pltpu.CompilerParams(vmem_limit_bytes=8 << 20),
    )(new_walkers, energy)
    return new_walkers, energy.reshape(32)


def solution(mesh):
    in_specs = (
        P("chol", "orb", None, None),
        P("chol", "orb", None),
        P("walker", "orb", None),
        P("walker", "orb", None),
        P("chol", "walker"),
    )
    out_specs = (P("walker", "orb", None), P("walker"))
    return jax.shard_map(
        per_device, mesh=mesh, in_specs=in_specs, out_specs=out_specs, check_vma=False
    )
```

```python
import functools

import jax
import jax.numpy as jnp
from jax import lax
from jax.experimental import pallas as pl
from jax.experimental.pallas import tpu as pltpu
from jax.sharding import PartitionSpec as P

NORB = 256
NOCC = 128
BLOCK = 64
TAYLOR = 4
SIDE = 4
F32 = jnp.float32
BF16 = jnp.bfloat16
MESH = pl.DeviceIdType.MESH
HALF = 64
WAY = (1, 3)


def swap_halves(x):
    return jnp.concatenate([x[:, BLOCK:], x[:, :BLOCK]], axis=1)


def kernel(
    step_factor, v_hbm, cols_hbm, g_hbm, w_hbm, f_hbm, out, e_ref,
    vbuf, vt, gbuf, gp, cbuf, fbuf, wbuf, tbuf, fx, fxr,
    pp, opp1, fin1, s1, last, pot, nw, esend, ebuf,
    lsem, ssem, rsem,
):
    chip = lax.axis_index("chol")
    core = lax.axis_index("orb")
    other = 1 - core
    px, py = chip // SIDE, chip % SIDE

    def chip_at(dx, dy):
        return ((px + dx) % SIDE) * SIDE + (py + dy) % SIDE

    def chip_of(h, da, db):
        return chip_at(da, db) if h == 0 else chip_at(db, da)

    def walker(h, da, db):
        return 2 * chip_of(h, da, db) + h

    def dev(c, k):
        return {"chol": c, "orb": k}

    used = [0]

    def slots(n=1):
        used[0] += n
        return used[0] - n

    def remote(src, dst, to, ridx, small=0):
        return pltpu.make_async_remote_copy(
            src_ref=src, dst_ref=dst, send_sem=ssem.at[small], recv_sem=rsem.at[ridx],
            device_id=to, device_id_type=MESH,
        )

    def send(src, dst, to, ridx, small=0):
        remote(src, dst, to, ridx, small).start()

    def arrive(dst, ridx):
        remote(dst, dst, dev(chip, other), ridx).wait_recv()

    barrier = pltpu.get_barrier_semaphore()
    partners = [dev(chip, other)]
    for dx, dy in ((1, 0), (3, 0), (2, 0), (0, 1), (0, 3), (0, 2)):
        partners += [dev(chip_at(dx, dy), core), dev(chip_at(dx, dy), other)]
    for to in partners:
        pl.semaphore_signal(barrier, inc=1, device_id=to, device_id_type=MESH)

    def load_g(n):
        rows = pl.ds(n * 16, 16)
        return pltpu.make_async_copy(g_hbm.at[:, rows, :], gbuf.at[:, rows, :], lsem.at[8 + n])

    def load_v(r, ii):
        n = r * 4 + ii
        return pltpu.make_async_copy(v_hbm.at[:, r, pl.ds(ii * 16, 16), :], vbuf.at[n], lsem.at[n])

    for r in range(2):
        for ii in range(4):
            load_g(r * 4 + ii).start()
            load_v(r, ii).start()
    fcopy = pltpu.make_async_copy(f_hbm, fbuf, lsem.at[16])
    fcopy.start()
    ccopy = pltpu.make_async_copy(cols_hbm, cbuf, lsem.at[17])
    ccopy.start()
    wcopy = pltpu.make_async_copy(w_hbm.at[pl.ds(2 * chip, 2)], wbuf, lsem.at[18])
    wcopy.start()

    low = lax.broadcasted_iota(jnp.int32, (16, 128), 1) < BLOCK
    own_at = pl.multiple_of(core * 128, 128)
    far_at = pl.multiple_of(other * 128, 128)
    for r in range(2):

        @pl.loop(0, 4)
        def _(ii):
            load_g(r * 4 + ii).wait()
            load_v(r, ii).wait()
            rows = pl.ds(pl.multiple_of(r * 64 + ii * 16, 16), 16)
            k0 = pl.multiple_of(ii * 2048, 2048)
            for w0 in (0, 16):
                near = jnp.swapaxes(gbuf[w0:w0 + 16, rows, pl.ds(own_at, 128)], 0, 1)
                far = jnp.swapaxes(gbuf[w0:w0 + 16, rows, pl.ds(far_at, 128)], 0, 1)
                for i in range(16):
                    a, b = near[i], far[i]
                    if r == 1:
                        a = swap_halves(a)
                    z = jnp.zeros_like(a)
                    choices = (jnp.where(low, a, z), a, jnp.where(low, a, swap_halves(b)), jnp.where(low, a, b))
                    for c, val in enumerate(choices):
                        gp[r, c * 32 + w0:c * 32 + w0 + 16, pl.ds(k0 + i * 128, 128)] = val
            for g0 in range(0, 256, 16):
                y = jnp.swapaxes(vbuf[r * 4 + ii, g0:g0 + 16, :, :], 0, 1)
                for i in range(16):
                    vt[r, g0:g0 + 16, pl.ds(k0 + i * 128, 128)] = y[i]

    fcopy.wait()
    ccopy.wait()
    wcopy.wait()
    masks = []
    partial = jnp.zeros((32, 256), F32)
    for r in range(2):
        acc = lax.dot_general(vt[r], gp[r], (((1,), (1,)), ((), ())), preferred_element_type=F32).T
        code = cbuf[r, 1:2, :]
        wanted = (4, 2 * core + (1 - r), 2 * other, 2 * other + 1)
        ms = [code == k for k in wanted]
        masks.append(ms)
        for c in range(4):
            partial = partial + jnp.where(ms[c], acc[c * 32:(c + 1) * 32], 0.0)
    fx[...] = partial
    tbuf[core] = wbuf[core]
    fi, wi = slots(), slots()
    pl.semaphore_wait(barrier, len(partners))
    send(fx, fxr, dev(chip, other), fi)
    send(wbuf.at[other], tbuf.at[core], dev(chip, other), wi)
    arrive(fxr, fi)
    bias = partial + fxr[...]
    shifted = fbuf[...] - bias

    local = 0.5 * jnp.sum(bias * bias, axis=1, keepdims=True)
    diag = lax.broadcasted_iota(jnp.int32, (32, 128), 0) == lax.broadcasted_iota(jnp.int32, (32, 128), 1)
    row = jnp.sum(jnp.where(diag, local, 0.0), axis=0, keepdims=True)
    esend[0] = jnp.broadcast_to(row, (8, 128))
    ex, ey = slots(), slots()
    for d in (1, 2, 3):
        send(esend.at[0], ebuf.at[0, d], dev(chip_at(d, 0), core), ex, 1)

    lo32 = lax.broadcasted_iota(jnp.int32, (32, 128), 1) < BLOCK
    o1 = {(h, d, r): slots() for h in range(2) for d in range(4) for r in range(2)}
    f1 = {(h, d, r): slots() for h in range(2) for d in (1, 2, 3) for r in range(2)}
    fl = [slots(), slots()]

    def rows_of(r, q):
        return pl.ds(r * HALF + q * 32, 32)

    def send_opp(d, r, q):
        for h in range(2):
            src = pp.at[walker(h, 2, d), rows_of(r, q)]
            send(src, opp1.at[h, d, r, q], dev(chip_of(h, WAY[q], 0), core), o1[h, d, r])

    def send_target(d, r, q, s):
        for h in range(2):
            src = pp.at[walker(h, WAY[s], d), rows_of(r, q)]
            if d == 0:
                send(src, last.at[core * 5 + s, rows_of(r, q)], dev(chip_of(h, WAY[s], 0), h), fl[r])
            else:
                send(src, fin1.at[h, d, r, s, q], dev(chip_of(h, WAY[s], 0), core), f1[h, d, r])

    def send_own(d, r):
        for s in range(2):
            send_target(d, r, 1 - s, s)

    def add_opp(d, r):
        for h in range(2):
            arrive(opp1.at[h, d, r], o1[h, d, r])
            for q in range(2):
                w = walker(h, WAY[q], d)
                pp[w, rows_of(r, q)] = (pp[w, rows_of(r, q)].astype(F32) + opp1[h, d, r, q].astype(F32)).astype(BF16)
        for s in range(2):
            send_target(d, r, s, s)

    for r in range(2):
        parts = [shifted] + [jnp.where(masks[r][c], shifted, 0.0) for c in (1, 2, 3)]
        lhs = jnp.concatenate(parts, axis=0).astype(BF16)

        def part(ii):
            k0 = pl.multiple_of(ii * 2048, 2048)
            o = jnp.dot(lhs, vt[r, :, pl.ds(k0, 2048)], preferred_element_type=F32)
            x0, x1 = [], []
            for i in range(16):
                t = o[:, i * 128:(i + 1) * 128]
                x0.append(jnp.where(lo32, t[0:32], t[32:64]).astype(BF16))
                x1.append(jnp.where(lo32, pltpu.roll(t[64:96], 64, 1), t[96:128]).astype(BF16))
            i0 = pl.multiple_of(r * 64 + ii * 16, 16)
            for wh in range(2):
                for side, x in ((0, x0), (1, x1)):
                    s = jnp.stack([q[wh * 16:(wh + 1) * 16] for q in x], axis=0)
                    pp[wh * 16:(wh + 1) * 16, pl.ds(i0, 16), side * 128:(side + 1) * 128] = jnp.swapaxes(s, 0, 1)

        for q in range(2):
            pl.loop(2 * q, 2 * q + 2)(part)
            for d in (2, 1, 3) if r else (2, 1, 3, 0):
                send_opp(d, r, q)
        for d in (2, 1) if r else (2, 1, 3, 0):
            send_own(d, r)
        rows = pl.ds(r * HALF, HALF)
        send(pp.at[2 * chip + other, rows], last.at[10, rows], dev(chip, other), fl[r])

    arrive(ebuf.at[0, pl.ds(1, 3)], ex)
    ebuf[0, 0] = esend[0]
    row = ordered_sum(ebuf, 0, px)
    esend[1] = row
    for d in (1, 2, 3):
        send(esend.at[1], ebuf.at[1, d], dev(chip_at(0, d), core), ey, 1)

    def finish(d, r):
        rows = pl.ds(r * HALF, HALF)
        for h in range(2):
            arrive(fin1.at[h, d, r], f1[h, d, r])
            both = fin1[h, d, r, 0].astype(F32) + fin1[h, d, r, 1].astype(F32)
            s1[h, d, r] = (pp[walker(h, 0, d), rows].astype(F32) + both.reshape(HALF, 256)).astype(BF16)
            send(s1.at[h, d, r], last.at[core * 5 + 1 + d, rows], dev(chip_of(h, 0, d), h), fl[r])

    for d in (2, 1, 3):
        add_opp(d, 0)
    send_own(3, 1)
    add_opp(0, 0)
    for q in range(2):
        send_opp(0, 1, q)
    send_own(0, 1)
    for d in (2, 1, 3):
        add_opp(d, 1)
    for d in (2, 1, 3):
        finish(d, 0)
    add_opp(0, 1)
    for d in (2, 1, 3):
        finish(d, 1)

    arrive(ebuf.at[1, pl.ds(1, 3)], ey)
    ebuf[1, 0] = esend[1]
    row = ordered_sum(ebuf, 1, py)
    e_ref[...] = row[0:1, 0:32]

    mine = 2 * chip + core
    for r in range(2):
        rows = pl.ds(r * HALF, HALF)
        arrive(last.at[:, rows], fl[r])
        for o in range(2):
            own = jnp.where(core == o, pp[mine, rows].astype(F32), last[10, rows].astype(F32))
            for n in range(5):
                own = own + last[o * 5 + n, rows].astype(F32)
            full = step_factor * own
            near, far = full[:, :128], full[:, 128:]
            if r == 1:
                near = pltpu.roll(near, BLOCK, 1)
            pair = [near, far] if o == 0 else [far, near]
            pot[pl.ds(o * 128 + r * HALF, HALF), :] = jnp.concatenate(pair, axis=1).astype(BF16)
    arrive(tbuf.at[other], wi)
    start = tbuf[...].reshape(NORB, NOCC)
    term = start
    total = jnp.zeros((NORB, NOCC), F32)
    for degree in range(1, TAYLOR + 1):
        product = jnp.dot(pot[...], term, preferred_element_type=F32)
        term = (product / degree).astype(BF16)
        total = total + term.astype(F32)
    nw[...] = (start.astype(F32) + total).astype(BF16).reshape(2, 128, NOCC)

    g1 = slots(6)
    g2 = slots()
    for d in (1, 3, 2):
        for o in range(2):
            to = dev(chip_at(core * d, other * d), o)
            send(nw.at[o], out.at[mine], to, g1 + core * 3 + d - 1, 0 if d == 2 else 2)
    send(nw.at[other], out.at[mine], dev(chip, other), g2)
    keep = pltpu.make_async_copy(nw.at[core], out.at[mine], lsem.at[0])
    keep.start()
    sent_first = pl.ds(0, 32)
    pltpu.make_async_copy(vbuf.at[0, sent_first], vbuf.at[1, sent_first], ssem.at[2]).wait()
    for d in (2, 1, 3):
        for o in range(2):
            send(nw.at[o], out.at[mine], dev(chip_at(other * d, core * d), o), g2)
    for d in (1, 3, 2):
        for h in range(2):
            w = walker(h, 0, 4 - d)
            arrive(out.at[w], g1 + h * 3 + d - 1)
            for da in (2, 1, 3):
                send(out.at[w], out.at[w], dev(chip_of(h, da, 0), core), g2)
    keep.wait()
    arrive(out.at[pl.ds(0, 25)], g2)
    whole = pl.ds(0, 182)
    pltpu.make_async_copy(vbuf.at[pl.ds(0, 4), whole], vbuf.at[pl.ds(4, 4), whole], ssem.at[0]).wait()
    pltpu.make_async_copy(ebuf.at[:, pl.ds(0, 3)], ebuf.at[:, pl.ds(1, 3)], ssem.at[1]).wait()
    assert used[0] == SEMS, used[0]


def ordered_sum(ebuf, stage, at):
    rows = [ebuf[stage, (at - q + SIDE) % SIDE] for q in range(SIDE)]
    return (rows[0] + rows[1]) + (rows[2] + rows[3])


SEMS = 41


def write_out(w_ref, e_ref, w_out, e_out, sem):
    copies = [
        pltpu.make_async_copy(w_ref, w_out, sem.at[0]),
        pltpu.make_async_copy(e_ref, e_out, sem.at[1]),
    ]
    for c in copies:
        c.start()
    for c in copies:
        c.wait()


def per_device(chol_vals, chol_cols, greens, walkers, fields):
    vectors = chol_vals.shape[0]
    step_factor = 72.0 / float(vectors * lax.axis_size("chol") * BLOCK) ** 0.5
    vmem = pltpu.VMEM
    hbm = pl.BlockSpec(memory_space=pltpu.HBM)
    new_walkers, energy = pl.pallas_call(
        functools.partial(kernel, step_factor),
        out_shape=(
            jax.ShapeDtypeStruct((32, 128, NOCC), BF16),
            jax.ShapeDtypeStruct((1, 32), F32),
        ),
        in_specs=[hbm] * 5,
        out_specs=(pl.BlockSpec(memory_space=pl.ANY), pl.BlockSpec(memory_space=vmem)),
        scratch_shapes=[
            vmem((8, 256, 16, 128), BF16),
            vmem((2, 256, 64 * 128), BF16),
            vmem((32, 128, 256), BF16),
            vmem((2, 128, 64 * 128), BF16),
            vmem((2, 2, 256), jnp.int32),
            vmem((32, 256), F32),
            vmem((2, 128, NOCC), BF16),
            vmem((2, 128, NOCC), BF16),
            vmem((32, 256), F32),
            vmem((32, 256), F32),
            vmem((32, 128, 256), BF16),
            vmem((2, 4, 2, 2, 32, 256), BF16),
            vmem((2, 4, 2, 2, 2, 32, 256), BF16),
            vmem((2, 4, 2, HALF, 256), BF16),
            vmem((11, 128, 256), BF16),
            vmem((NORB, NORB), BF16),
            vmem((2, 128, NOCC), BF16),
            vmem((2, 8, 128), F32),
            vmem((2, SIDE, 8, 128), F32),
            pltpu.SemaphoreType.DMA((19,)),
            pltpu.SemaphoreType.DMA((3,)),
            pltpu.SemaphoreType.DMA((SEMS,)),
        ],
        compiler_params=pltpu.CompilerParams(
            collective_id=0, has_side_effects=True, vmem_limit_bytes=44 << 20
        ),
    )(*[pltpu.with_memory_space_constraint(a, pltpu.HBM) for a in (chol_vals, chol_cols.transpose(1, 2, 0), greens, walkers, fields.T)])
    in_vmem = pl.BlockSpec(memory_space=pl.ANY)
    new_walkers, energy = pl.pallas_call(
        write_out,
        out_shape=(
            jax.ShapeDtypeStruct((32, 128, NOCC), BF16),
            jax.ShapeDtypeStruct((1, 32), F32),
        ),
        in_specs=[in_vmem, in_vmem],
        out_specs=(hbm, hbm),
        scratch_shapes=[pltpu.SemaphoreType.DMA((2,))],
        compiler_params=pltpu.CompilerParams(vmem_limit_bytes=8 << 20),
    )(new_walkers, energy)
    return new_walkers, energy.reshape(32)


def solution(mesh):
    in_specs = (
        P("chol", "orb", None, None),
        P("chol", "orb", None),
        P("walker", "orb", None),
        P("walker", "orb", None),
        P("chol", "walker"),
    )
    out_specs = (P("walker", "orb", None), P("walker"))
    return jax.shard_map(
        per_device, mesh=mesh, in_specs=in_specs, out_specs=out_specs, check_vma=False
    )
```

```python
import functools

import jax
import jax.numpy as jnp
from jax import lax
from jax.experimental import pallas as pl
from jax.experimental.pallas import tpu as pltpu
from jax.sharding import PartitionSpec as P

NORB = 256
NOCC = 128
BLOCK = 64
TAYLOR = 4
SIDE = 4
F32 = jnp.float32
BF16 = jnp.bfloat16
MESH = pl.DeviceIdType.MESH
HALF = 64
WAY = (1, 3)


def swap_halves(x):
    return jnp.concatenate([x[:, BLOCK:], x[:, :BLOCK]], axis=1)


def kernel(
    step_factor, v_hbm, cols_hbm, g_hbm, w_hbm, f_hbm, out, e_ref,
    vbuf, vt, gbuf, gp, cbuf, fbuf, wbuf, tbuf, fx, fxr,
    pp, opp1, fin1, s1, last, pot, nw, esend, ebuf,
    lsem, ssem, rsem,
):
    chip = lax.axis_index("chol")
    core = lax.axis_index("orb")
    other = 1 - core
    px, py = chip // SIDE, chip % SIDE

    def chip_at(dx, dy):
        return ((px + dx) % SIDE) * SIDE + (py + dy) % SIDE

    def chip_of(h, da, db):
        return chip_at(da, db) if h == 0 else chip_at(db, da)

    def walker(h, da, db):
        return 2 * chip_of(h, da, db) + h

    def dev(c, k):
        return {"chol": c, "orb": k}

    used = [0]

    def slots(n=1):
        used[0] += n
        return used[0] - n

    def remote(src, dst, to, ridx, small=0):
        return pltpu.make_async_remote_copy(
            src_ref=src, dst_ref=dst, send_sem=ssem.at[small], recv_sem=rsem.at[ridx],
            device_id=to, device_id_type=MESH,
        )

    def send(src, dst, to, ridx, small=0):
        remote(src, dst, to, ridx, small).start()

    def arrive(dst, ridx):
        remote(dst, dst, dev(chip, other), ridx).wait_recv()

    barrier = pltpu.get_barrier_semaphore()
    partners = [dev(chip, other)]
    for dx, dy in ((1, 0), (3, 0), (2, 0), (0, 1), (0, 3), (0, 2)):
        partners += [dev(chip_at(dx, dy), core), dev(chip_at(dx, dy), other)]
    for to in partners:
        pl.semaphore_signal(barrier, inc=1, device_id=to, device_id_type=MESH)

    def load_g(n):
        rows = pl.ds(n * 16, 16)
        return pltpu.make_async_copy(g_hbm.at[:, rows, :], gbuf.at[:, rows, :], lsem.at[8 + n])

    def load_v(r, ii):
        n = r * 4 + ii
        return pltpu.make_async_copy(v_hbm.at[:, r, pl.ds(ii * 16, 16), :], vbuf.at[n], lsem.at[n])

    for r in range(2):
        for ii in range(4):
            load_g(r * 4 + ii).start()
            load_v(r, ii).start()
    fcopy = pltpu.make_async_copy(f_hbm, fbuf, lsem.at[16])
    fcopy.start()
    ccopy = pltpu.make_async_copy(cols_hbm, cbuf, lsem.at[17])
    ccopy.start()
    wcopy = pltpu.make_async_copy(w_hbm.at[pl.ds(2 * chip, 2)], wbuf, lsem.at[18])
    wcopy.start()

    low = lax.broadcasted_iota(jnp.int32, (16, 128), 1) < BLOCK
    own_at = pl.multiple_of(core * 128, 128)
    far_at = pl.multiple_of(other * 128, 128)
    for r in range(2):

        @pl.loop(0, 4)
        def _(ii):
            load_g(r * 4 + ii).wait()
            load_v(r, ii).wait()
            rows = pl.ds(pl.multiple_of(r * 64 + ii * 16, 16), 16)
            k0 = pl.multiple_of(ii * 2048, 2048)
            for w0 in (0, 16):
                near = jnp.swapaxes(gbuf[w0:w0 + 16, rows, pl.ds(own_at, 128)], 0, 1)
                far = jnp.swapaxes(gbuf[w0:w0 + 16, rows, pl.ds(far_at, 128)], 0, 1)
                for i in range(16):
                    a, b = near[i], far[i]
                    if r == 1:
                        a = swap_halves(a)
                    z = jnp.zeros_like(a)
                    choices = (jnp.where(low, a, z), a, jnp.where(low, a, swap_halves(b)), jnp.where(low, a, b))
                    for c, val in enumerate(choices):
                        gp[r, c * 32 + w0:c * 32 + w0 + 16, pl.ds(k0 + i * 128, 128)] = val
            for g0 in range(0, 256, 16):
                y = jnp.swapaxes(vbuf[r * 4 + ii, g0:g0 + 16, :, :], 0, 1)
                for i in range(16):
                    vt[r, g0:g0 + 16, pl.ds(k0 + i * 128, 128)] = y[i]

    fcopy.wait()
    ccopy.wait()
    wcopy.wait()
    masks = []
    partial = jnp.zeros((32, 256), F32)
    for r in range(2):
        acc = lax.dot_general(vt[r], gp[r], (((1,), (1,)), ((), ())), preferred_element_type=F32).T
        code = cbuf[r, 1:2, :]
        wanted = (4, 2 * core + (1 - r), 2 * other, 2 * other + 1)
        ms = [code == k for k in wanted]
        masks.append(ms)
        for c in range(4):
            partial = partial + jnp.where(ms[c], acc[c * 32:(c + 1) * 32], 0.0)
    fx[...] = partial
    tbuf[core] = wbuf[core]
    fi, wi = slots(), slots()
    pl.semaphore_wait(barrier, len(partners))
    send(fx, fxr, dev(chip, other), fi)
    send(wbuf.at[other], tbuf.at[core], dev(chip, other), wi)
    arrive(fxr, fi)
    bias = partial + fxr[...]
    shifted = fbuf[...] - bias

    local = 0.5 * jnp.sum(bias * bias, axis=1, keepdims=True)
    diag = lax.broadcasted_iota(jnp.int32, (32, 128), 0) == lax.broadcasted_iota(jnp.int32, (32, 128), 1)
    row = jnp.sum(jnp.where(diag, local, 0.0), axis=0, keepdims=True)
    esend[0] = jnp.broadcast_to(row, (8, 128))
    ex, ey = slots(), slots()
    for d in (1, 2, 3):
        send(esend.at[0], ebuf.at[0, d], dev(chip_at(d, 0), core), ex, 1)

    lo32 = lax.broadcasted_iota(jnp.int32, (32, 128), 1) < BLOCK
    o1 = {(h, d, r): slots() for h in range(2) for d in range(4) for r in range(2)}
    f1 = {(h, d, r): slots() for h in range(2) for d in (1, 2, 3) for r in range(2)}
    fl = [slots(), slots()]

    def rows_of(r, q):
        return pl.ds(r * HALF + q * 32, 32)

    def send_opp(d, r, q):
        for h in range(2):
            src = pp.at[walker(h, 2, d), rows_of(r, q)]
            send(src, opp1.at[h, d, r, q], dev(chip_of(h, WAY[q], 0), core), o1[h, d, r])

    def send_target(d, r, q, s):
        for h in range(2):
            src = pp.at[walker(h, WAY[s], d), rows_of(r, q)]
            if d == 0:
                send(src, last.at[core * 5 + s, rows_of(r, q)], dev(chip_of(h, WAY[s], 0), h), fl[r])
            else:
                send(src, fin1.at[h, d, r, s, q], dev(chip_of(h, WAY[s], 0), core), f1[h, d, r])

    def send_own(d, r):
        for s in range(2):
            send_target(d, r, 1 - s, s)

    def add_opp(d, r):
        for h in range(2):
            arrive(opp1.at[h, d, r], o1[h, d, r])
            for q in range(2):
                w = walker(h, WAY[q], d)
                pp[w, rows_of(r, q)] = (pp[w, rows_of(r, q)].astype(F32) + opp1[h, d, r, q].astype(F32)).astype(BF16)
        for s in range(2):
            send_target(d, r, s, s)

    for r in range(2):
        parts = [shifted] + [jnp.where(masks[r][c], shifted, 0.0) for c in (1, 2, 3)]
        lhs = jnp.concatenate(parts, axis=0).astype(BF16)

        def part(ii):
            k0 = pl.multiple_of(ii * 2048, 2048)
            o = jnp.dot(lhs, vt[r, :, pl.ds(k0, 2048)], preferred_element_type=F32)
            x0, x1 = [], []
            for i in range(16):
                t = o[:, i * 128:(i + 1) * 128]
                x0.append(jnp.where(lo32, t[0:32], t[32:64]).astype(BF16))
                x1.append(jnp.where(lo32, pltpu.roll(t[64:96], 64, 1), t[96:128]).astype(BF16))
            i0 = pl.multiple_of(r * 64 + ii * 16, 16)
            for wh in range(2):
                for side, x in ((0, x0), (1, x1)):
                    s = jnp.stack([q[wh * 16:(wh + 1) * 16] for q in x], axis=0)
                    pp[wh * 16:(wh + 1) * 16, pl.ds(i0, 16), side * 128:(side + 1) * 128] = jnp.swapaxes(s, 0, 1)

        for q in range(2):
            pl.loop(2 * q, 2 * q + 2)(part)
            for d in (2, 1, 3) if r else (2, 1, 3, 0):
                send_opp(d, r, q)
        for d in (2, 1) if r else (2, 1, 3, 0):
            send_own(d, r)
        rows = pl.ds(r * HALF, HALF)
        send(pp.at[2 * chip + other, rows], last.at[10, rows], dev(chip, other), fl[r])

    arrive(ebuf.at[0, pl.ds(1, 3)], ex)
    ebuf[0, 0] = esend[0]
    row = ordered_sum(ebuf, 0, px)
    esend[1] = row
    for d in (1, 2, 3):
        send(esend.at[1], ebuf.at[1, d], dev(chip_at(0, d), core), ey, 1)

    def finish(d, r):
        rows = pl.ds(r * HALF, HALF)
        for h in range(2):
            arrive(fin1.at[h, d, r], f1[h, d, r])
            both = fin1[h, d, r, 0].astype(F32) + fin1[h, d, r, 1].astype(F32)
            s1[h, d, r] = (pp[walker(h, 0, d), rows].astype(F32) + both.reshape(HALF, 256)).astype(BF16)
            send(s1.at[h, d, r], last.at[core * 5 + 1 + d, rows], dev(chip_of(h, 0, d), h), fl[r])

    for d in (2, 1, 3):
        add_opp(d, 0)
    send_own(3, 1)
    add_opp(0, 0)
    for q in range(2):
        send_opp(0, 1, q)
    send_own(0, 1)
    for d in (2, 1, 3):
        add_opp(d, 1)
    for d in (2, 1, 3):
        finish(d, 0)
    add_opp(0, 1)
    for d in (2, 1, 3):
        finish(d, 1)

    arrive(ebuf.at[1, pl.ds(1, 3)], ey)
    ebuf[1, 0] = esend[1]
    row = ordered_sum(ebuf, 1, py)
    e_ref[...] = row[0:1, 0:32]

    mine = 2 * chip + core
    arrive(tbuf.at[other], wi)
    start = tbuf[...].reshape(NORB, NOCC)
    first_rows = {}
    for r in range(2):
        rows = pl.ds(r * HALF, HALF)
        arrive(last.at[:, rows], fl[r])
        for o in range(2):
            own = jnp.where(core == o, pp[mine, rows].astype(F32), last[10, rows].astype(F32))
            for n in range(5):
                own = own + last[o * 5 + n, rows].astype(F32)
            full = step_factor * own
            near, far = full[:, :128], full[:, 128:]
            if r == 1:
                near = pltpu.roll(near, BLOCK, 1)
            pair = [near, far] if o == 0 else [far, near]
            piece = jnp.concatenate(pair, axis=1).astype(BF16)
            pot[pl.ds(o * 128 + r * HALF, HALF), :] = piece
            first_rows[o, r] = jnp.dot(piece, start, preferred_element_type=F32)
    term = start
    total = jnp.zeros((NORB, NOCC), F32)
    for degree in range(1, TAYLOR + 1):
        if degree == 1:
            product = jnp.concatenate([first_rows[o, r] for o in range(2) for r in range(2)], axis=0)
        else:
            product = jnp.dot(pot[...], term, preferred_element_type=F32)
        term = (product / degree).astype(BF16)
        total = total + term.astype(F32)
    nw[...] = (start.astype(F32) + total).astype(BF16).reshape(2, 128, NOCC)

    g1 = slots(6)
    g2 = slots()
    for d in (1, 3, 2):
        for o in range(2):
            to = dev(chip_at(core * d, other * d), o)
            send(nw.at[o], out.at[mine], to, g1 + core * 3 + d - 1, 0 if d == 2 else 2)
    send(nw.at[other], out.at[mine], dev(chip, other), g2)
    keep = pltpu.make_async_copy(nw.at[core], out.at[mine], lsem.at[0])
    keep.start()
    sent_first = pl.ds(0, 32)
    pltpu.make_async_copy(vbuf.at[0, sent_first], vbuf.at[1, sent_first], ssem.at[2]).wait()
    for d in (2, 1, 3):
        for o in range(2):
            send(nw.at[o], out.at[mine], dev(chip_at(other * d, core * d), o), g2)
    for d in (1, 3, 2):
        for h in range(2):
            w = walker(h, 0, 4 - d)
            arrive(out.at[w], g1 + h * 3 + d - 1)
            for da in (2, 1, 3):
                send(out.at[w], out.at[w], dev(chip_of(h, da, 0), core), g2)
    keep.wait()
    arrive(out.at[pl.ds(0, 25)], g2)
    whole = pl.ds(0, 182)
    pltpu.make_async_copy(vbuf.at[pl.ds(0, 4), whole], vbuf.at[pl.ds(4, 4), whole], ssem.at[0]).wait()
    pltpu.make_async_copy(ebuf.at[:, pl.ds(0, 3)], ebuf.at[:, pl.ds(1, 3)], ssem.at[1]).wait()
    assert used[0] == SEMS, used[0]


def ordered_sum(ebuf, stage, at):
    rows = [ebuf[stage, (at - q + SIDE) % SIDE] for q in range(SIDE)]
    return (rows[0] + rows[1]) + (rows[2] + rows[3])


SEMS = 41


def write_out(w_ref, e_ref, w_out, e_out, sem):
    copies = [
        pltpu.make_async_copy(w_ref, w_out, sem.at[0]),
        pltpu.make_async_copy(e_ref, e_out, sem.at[1]),
    ]
    for c in copies:
        c.start()
    for c in copies:
        c.wait()


def per_device(chol_vals, chol_cols, greens, walkers, fields):
    vectors = chol_vals.shape[0]
    step_factor = 72.0 / float(vectors * lax.axis_size("chol") * BLOCK) ** 0.5
    vmem = pltpu.VMEM
    hbm = pl.BlockSpec(memory_space=pltpu.HBM)
    new_walkers, energy = pl.pallas_call(
        functools.partial(kernel, step_factor),
        out_shape=(
            jax.ShapeDtypeStruct((32, 128, NOCC), BF16),
            jax.ShapeDtypeStruct((1, 32), F32),
        ),
        in_specs=[hbm] * 5,
        out_specs=(pl.BlockSpec(memory_space=pl.ANY), pl.BlockSpec(memory_space=vmem)),
        scratch_shapes=[
            vmem((8, 256, 16, 128), BF16),
            vmem((2, 256, 64 * 128), BF16),
            vmem((32, 128, 256), BF16),
            vmem((2, 128, 64 * 128), BF16),
            vmem((2, 2, 256), jnp.int32),
            vmem((32, 256), F32),
            vmem((2, 128, NOCC), BF16),
            vmem((2, 128, NOCC), BF16),
            vmem((32, 256), F32),
            vmem((32, 256), F32),
            vmem((32, 128, 256), BF16),
            vmem((2, 4, 2, 2, 32, 256), BF16),
            vmem((2, 4, 2, 2, 2, 32, 256), BF16),
            vmem((2, 4, 2, HALF, 256), BF16),
            vmem((11, 128, 256), BF16),
            vmem((NORB, NORB), BF16),
            vmem((2, 128, NOCC), BF16),
            vmem((2, 8, 128), F32),
            vmem((2, SIDE, 8, 128), F32),
            pltpu.SemaphoreType.DMA((19,)),
            pltpu.SemaphoreType.DMA((3,)),
            pltpu.SemaphoreType.DMA((SEMS,)),
        ],
        compiler_params=pltpu.CompilerParams(
            collective_id=0, has_side_effects=True, vmem_limit_bytes=44 << 20
        ),
    )(*[pltpu.with_memory_space_constraint(a, pltpu.HBM) for a in (chol_vals, chol_cols.transpose(1, 2, 0), greens, walkers, fields.T)])
    in_vmem = pl.BlockSpec(memory_space=pl.ANY)
    new_walkers, energy = pl.pallas_call(
        write_out,
        out_shape=(
            jax.ShapeDtypeStruct((32, 128, NOCC), BF16),
            jax.ShapeDtypeStruct((1, 32), F32),
        ),
        in_specs=[in_vmem, in_vmem],
        out_specs=(hbm, hbm),
        scratch_shapes=[pltpu.SemaphoreType.DMA((2,))],
        compiler_params=pltpu.CompilerParams(vmem_limit_bytes=8 << 20),
    )(new_walkers, energy)
    return new_walkers, energy.reshape(32)


def solution(mesh):
    in_specs = (
        P("chol", "orb", None, None),
        P("chol", "orb", None),
        P("walker", "orb", None),
        P("walker", "orb", None),
        P("chol", "walker"),
    )
    out_specs = (P("walker", "orb", None), P("walker"))
    return jax.shard_map(
        per_device, mesh=mesh, in_specs=in_specs, out_specs=out_specs, check_vma=False
    )
```
